32 devices in a mesh: sa: 8 (over y, x, core), tp: 4 (over z).
Axes of the slice: x: 2, y: 2, z: 4, core: 2. Of those that a mesh axis runs over, the one named last changes fastest.
Arguments:
- window: float32 [2, 2, 16, 32, 512], P(None, None, 'sa', None, 'tp'), may hold values from -4 to 4
- damping: float32 [16, 32], P('sa'), may hold values from 0 to 1
- propagator: float32 [2, 32, 32], replicated, may hold values from -1 to 1, as said below
- coupling: float32 [32], replicated, may hold values from 0.5 to 1.5
Outputs:
- lesser_next: float32 [2, 16, 32, 512], P(None, 'sa', None, 'tp')
The draws below stay inside these ranges and needn't reach their ends.
Inputs may be any that keep to these rules, and one draw needn't show every extreme that they name: `propagator`: a unitary matrix.
All inputs are finite; a program needn't handle non-finite values.
Results may differ from the reference program's by a relative error of at most 0.0079.
Values may be sent and summed in bfloat16 or wider, within the bound.
A program may use at most 64 MiB of HBM per device.

```python
import math
import jax
import jax.numpy as jnp
from jax import lax

NO = 32
T_SIZE = 16


def draw_propagator(key, part):
    key_real = jax.random.fold_in(key, 11)
    key_imag = jax.random.fold_in(key, 12)
    sample_re = jax.random.normal(key_real, (NO, NO), jnp.float32)
    sample_im = jax.random.normal(key_imag, (NO, NO), jnp.float32)
    hermitian = ((sample_re + sample_re.T) * 0.5 + 1j * (sample_im - sample_im.T) * 0.5) * (1.5 / jnp.sqrt(NO * 1.0))
    identity = jnp.eye(NO, dtype=jnp.complex64)
    unitary = jnp.linalg.solve(identity + 0.5j * hermitian, identity - 0.5j * hermitian)
    return jnp.stack([jnp.real(unitary), jnp.imag(unitary)]).astype(jnp.float32)


def draw_damping(key, part):
    key_fast = jax.random.fold_in(key, 21)
    key_slow = jax.random.fold_in(key, 22)
    key_quick = jax.random.fold_in(key, 23)
    key_modulate = jax.random.fold_in(key, 24)
    key_spots = jax.random.fold_in(key, 25)
    key_factors = jax.random.fold_in(key, 26)
    fast_share = 0.5
    fast = jax.random.uniform(key_fast, (NO,), jnp.float32) < fast_share
    slow_rate = jax.random.uniform(key_slow, (NO,), jnp.float32, 0.05, 0.8) / T_SIZE
    quick_rate = jax.random.uniform(key_quick, (NO,), jnp.float32, 1.0 / 50.0, 1.0 / 30.0)
    relaxation_speeds = jnp.where(fast, quick_rate, slow_rate)
    forcing_envelope = jnp.exp(jax.random.uniform(key_modulate, (T_SIZE, 1), jnp.float32, -0.7, 0.7))
    excitation_locations = jax.random.randint(key_spots, (3,), 0, T_SIZE)
    amplitude_multipliers = jax.random.uniform(key_factors, (3,), jnp.float32, 0.6, 0.85)
    lattice_coordinates = jnp.arange(T_SIZE)[:, None]
    excitation_episodes = jnp.prod(jnp.where(lattice_coordinates == excitation_locations[None, :], amplitude_multipliers[None, :], 1.0), axis=1)
    return (jnp.exp(-relaxation_speeds[None, :] * forcing_envelope) * excitation_episodes[:, None]).astype(jnp.float32)


def block_scale(rng, extent, cuts, low, high):
    gain, own = 1.0, jax.random.fold_in(rng, 6)
    for dim, parts in cuts:
        steps = jnp.exp(jax.random.uniform(jax.random.fold_in(own, dim), (parts,), jnp.float32, low / len(cuts), high / len(cuts)))
        gain = gain * jnp.repeat(steps, extent[dim] // parts).reshape([-1 if axis == dim else 1 for axis in range(len(extent))])
    return gain


def centred(rng, shape, scale, reach, split=(), kind=jnp.bfloat16):
    drawn = jax.random.normal(rng, shape, jnp.float32) * scale
    if len(split) > 0:
        drawn = block_scale(rng, shape, split, -0.22, 0.18) * drawn
    return jnp.clip(drawn, min=-reach, max=reach).astype(kind)


def setup_inputs(seed: int = 0) -> dict:
    seeds = jax.random.split(jax.random.key(seed), 5)
    window = centred(seeds[0], (2, 2, T_SIZE, NO, T_SIZE * NO), 1.0, 4.0, ((2, 8), (4, 4)), jnp.float32)
    damping = draw_damping(jax.random.fold_in(seeds[4], 71), 0)
    propagator = draw_propagator(jax.random.fold_in(seeds[4], 71), 0)
    coupling = jnp.clip(jnp.exp(jax.random.uniform(seeds[3], (NO,), jnp.float32, math.log(0.5), math.log(1.5))), 0.5, 1.5)
    return dict(window=window, damping=damping, propagator=propagator, coupling=coupling)


highest = lax.Precision.HIGHEST

def spectral_self_energy(occupied_correlator, greater, coupling, column_tiles):
    factor = jnp.tile(coupling[:, None] * coupling[None, :], (1, column_tiles))
    less_re, less_im = (occupied_correlator[0], occupied_correlator[1])
    great_re, great_im = (greater[0], greater[1])
    lsquare_re = less_re * less_re - less_im * less_im
    lsquare_im = 2.0 * less_re * less_im
    gsquare_re = great_re * great_re - great_im * great_im
    gsquare_im = 2.0 * great_re * great_im
    sless_re = -factor * (lsquare_re * great_re + lsquare_im * great_im)
    sless_im = -factor * (lsquare_im * great_re - lsquare_re * great_im)
    sgreat_re = -factor * (gsquare_re * less_re + gsquare_im * less_im)
    sgreat_im = -factor * (gsquare_im * less_re - gsquare_re * less_im)
    return jnp.stack([sgreat_re - sless_re, sgreat_im - sless_im]).astype(jnp.bfloat16)

def complex_product(left_re, left_im, right_re, right_im):
    cosine_component = jnp.dot(left_re, right_re, precision=highest) - jnp.dot(left_im, right_im, precision=highest)
    imag_part = jnp.dot(left_re, right_im, precision=highest) + jnp.dot(left_im, right_re, precision=highest)
    return (cosine_component, imag_part)

def collision_term(spectral, history, weight_scale):
    width = spectral.shape[1] * spectral.shape[2]
    left_re = spectral[0].reshape(width, width)
    left_im = spectral[1].reshape(width, width)
    right_re = history[0].reshape(width, width)
    right_im = history[1].reshape(width, width)
    cosine_component = jnp.dot(left_re.astype(jnp.float32), right_re.astype(jnp.float32), preferred_element_type=jnp.float32) - jnp.dot(left_im.astype(jnp.float32), right_im.astype(jnp.float32), preferred_element_type=jnp.float32)
    imag_part = jnp.dot(left_re.astype(jnp.float32), right_im.astype(jnp.float32), preferred_element_type=jnp.float32) + jnp.dot(left_im.astype(jnp.float32), right_re.astype(jnp.float32), preferred_element_type=jnp.float32)
    return weight_scale * jnp.stack([cosine_component, imag_part]).reshape(history.shape)

def propagate(forcing, damping, propagator, initial):

    def advance(state, inputs):
        damp_row, force_row = inputs
        cosine_component, imag_part = complex_product(propagator[0], propagator[1], state[0], state[1])
        advanced = damp_row[None, :, None] * jnp.stack([cosine_component, imag_part]) + force_row
        return (advanced, advanced)
    last_state, produced = lax.scan(advance, initial, (damping, jnp.moveaxis(forcing, 1, 0)))
    return jnp.moveaxis(produced, 0, 1)

def reference(window, damping, propagator, coupling):
    occupied_correlator = window[0]
    greater = window[1]
    initial = occupied_correlator[:, 0]
    weight_scale = 1.0 / (T_SIZE * math.sqrt(NO))
    first_spectral = spectral_self_energy(occupied_correlator, greater, coupling, T_SIZE)
    first_term = collision_term(first_spectral, occupied_correlator.astype(jnp.bfloat16), weight_scale)
    predicted = propagate(first_term, damping, propagator, initial)
    second_spectral = spectral_self_energy(predicted, greater, coupling, T_SIZE)
    second_term = collision_term(second_spectral, predicted.astype(jnp.bfloat16), weight_scale)
    return propagate(0.5 * (first_term + second_term), damping, propagator, initial)
```

```python
import functools
import math

import jax
import jax.numpy as jnp
from jax import lax
from jax.experimental import pallas as pl
from jax.experimental.pallas import tpu as pltpu
from jax.sharding import PartitionSpec as P

MESH = pl.DeviceIdType.MESH
F32 = jnp.float32
BF16 = jnp.bfloat16


def exact(a, b):
    return jnp.dot(a, b, precision=lax.Precision.HIGHEST, preferred_element_type=F32)


def split(x):
    high = x.astype(BF16)
    return high, (x - high.astype(F32)).astype(BF16)


def mm(a, b):
    return jnp.dot(a, b, preferred_element_type=F32)


def mm3(a, b):
    return mm(a[0], b[0]) + (mm(a[0], b[1]) + mm(a[1], b[0]))


def spectral_of(x_re, x_im, g_re, g_im, factor):
    lsquare_re = x_re * x_re - x_im * x_im
    lsquare_im = 2.0 * x_re * x_im
    gsquare_re = g_re * g_re - g_im * g_im
    gsquare_im = 2.0 * g_re * g_im
    sless_re = -factor * (lsquare_re * g_re + lsquare_im * g_im)
    sless_im = -factor * (lsquare_im * g_re - lsquare_re * g_im)
    sgreat_re = -factor * (gsquare_re * x_re + gsquare_im * x_im)
    sgreat_im = -factor * (gsquare_im * x_re - gsquare_re * x_im)
    return jnp.concatenate([sgreat_re - sless_re, sgreat_im - sless_im], axis=0).astype(BF16)


def low_lanes(x):
    return lax.broadcasted_iota(jnp.int32, x.shape, 1) < x.shape[1] // 2


def swap(x):
    return pltpu.roll(x, x.shape[1] // 2, 1)


def signed(x):
    return jnp.where(low_lanes(x), -x, x)


def pack(re, im):
    low = low_lanes(re)
    return jnp.where(low, re, swap(im)), jnp.where(low, swap(re), im)


def joined(a, b):
    return a + signed(swap(b))


def split_parts(x, no):
    n = x.shape[0] // (2 * no)
    y = x.reshape(n, 2, no, x.shape[1])
    return y[:, 0].reshape(n * no, x.shape[1]), y[:, 1].reshape(n * no, x.shape[1])


def spectral_packed(x, g, factor):
    low = low_lanes(x)
    xs, gs = swap(x), swap(g)
    x_re, x_im = jnp.where(low, x, xs), jnp.where(low, xs, x)
    g_re, g_im = jnp.where(low, g, gs), jnp.where(low, gs, g)
    z = x * g_re - signed(xs * g_im)
    return factor * (z * (x_re + signed(g_re)) + swap(z) * (signed(x_im) - g_im))


def kernel(
    n_sa, n_tp, scale,
    win_in, damp_in, prop_in, coup_in, out,
    win, damp, prop, coup, s_in, dall, hist, spec1, gst, gall, fst, fall, pmat, s2, pst, ps, y2, yst,
    s_d, r_d, s_h, r_h, s_g, r_g, s_s, r_s, s_f, r_f, s_p, r_p, s_q, r_q, s_y, r_y,
):
    me_sa = lax.axis_index("sa")
    me_tp = lax.axis_index("tp")
    no = prop.shape[1]
    cols = win.shape[4]
    rows = win.shape[2] * no
    core = lax.rem(me_sa, 2)
    pair = lax.div(me_sa, 2)
    sib = pair * 2 + 1 - core

    barrier = pltpu.get_barrier_semaphore()
    for k in range(1, n_tp):
        who = lax.rem(me_tp + k, n_tp)
        pl.semaphore_signal(barrier, inc=1, device_id=(me_sa, who), device_id_type=MESH)
        pl.semaphore_signal(barrier, inc=1, device_id=(sib, who), device_id_type=MESH)
    for k in range(1, n_sa):
        pl.semaphore_signal(
            barrier, inc=1, device_id=(lax.rem(me_sa + k, n_sa), me_tp), device_id_type=MESH
        )

    loads = [
        pltpu.make_async_copy(src, dst, s_in.at[n])
        for n, (src, dst) in enumerate(
            [(win_in, win), (coup_in, coup), (damp_in, damp), (prop_in, prop)]
        )
    ]
    for load in loads:
        load.start()

    pending = []

    def remote(src, dst, send, recv, dev):
        return pltpu.make_async_remote_copy(
            src_ref=src, dst_ref=dst, send_sem=send, recv_sem=recv,
            device_id=dev, device_id_type=MESH,
        )

    def push(src, dst, send, recv, dev):
        copy = remote(src, dst, send, recv, dev)
        copy.start()
        pending.append(copy)

    def send_sa(buf, send, recv):
        for k in range(1, n_sa):
            who = lax.rem(me_sa + k, n_sa)
            push(buf.at[me_sa], buf.at[me_sa], send.at[k - 1], recv.at[me_sa], (who, me_tp))

    def send_half(src, buf, send, recv):
        for k in range(1, n_sa):
            who = lax.rem(me_sa + k, n_sa)
            push(src.at[lax.rem(who, 2)], buf.at[me_sa], send.at[k - 1], recv.at[me_sa], (who, me_tp))

    def wait_sa(buf, send, recv):
        for k in range(1, n_sa):
            who = lax.rem(me_sa + k, n_sa)
            remote(buf.at[who], buf.at[who], send.at[k - 1], recv.at[who], (who, me_tp)).wait_recv()

    for load in loads:
        load.wait()

    row_id = lax.broadcasted_iota(jnp.int32, (no, cols), 0)
    lane_id = lax.broadcasted_iota(jnp.int32, (no, cols), 1)
    tiled = (lax.rem(lane_id, no) == row_id).astype(F32)
    c_row = coup[...]
    c_lanes = exact(c_row, tiled)
    eye = lax.broadcasted_iota(jnp.int32, (no, no), 0) == lax.broadcasted_iota(jnp.int32, (no, no), 1)
    c_col = jnp.sum(jnp.where(eye, jnp.broadcast_to(c_row, (no, no)), 0.0), axis=1, keepdims=True)
    factor = c_col * c_lanes
    factor2 = jnp.concatenate([factor] * win.shape[2], axis=0)

    l_re = win[0, 0].reshape(rows, cols)
    l_im = win[0, 1].reshape(rows, cols)
    g_re = win[1, 0].reshape(rows, cols)
    g_im = win[1, 1].reshape(rows, cols)
    spec1[me_tp] = spectral_of(l_re, l_im, g_re, g_im, factor2)
    l0, l1 = pack(l_re, l_im)
    hmine = hist.at[me_sa]
    hmine[:, 0:cols] = l0.astype(BF16)
    hmine[:, cols:] = l1.astype(BF16)
    dmine = dall.at[me_sa]
    dmine[...] = jnp.zeros(dmine.shape, F32)
    dmine[0:2, 0:no] = damp[...]
    g0, g1 = pack(g_re, g_im)
    gst[0] = g0.astype(BF16)
    gst[1] = g1.astype(BF16)
    gall[me_sa] = gst[core]

    pl.semaphore_wait(barrier, n_sa - 1 + 2 * (n_tp - 1))
    for k in range(1, n_tp):
        who = lax.rem(me_tp + k, n_tp)
        push(spec1.at[me_tp], spec1.at[me_tp], s_s.at[k - 1], r_s.at[me_tp], (me_sa, who))
    send_sa(hist, s_h, r_h)
    send_sa(dall, s_d, r_d)
    send_half(gst, gall, s_g, r_g)

    first = (lax.broadcasted_iota(jnp.int32, (no, 2 * no), 0)
             == lax.broadcasted_iota(jnp.int32, (no, 2 * no), 1)).astype(F32)
    second = (lax.broadcasted_iota(jnp.int32, (no, 2 * no), 0) + no
              == lax.broadcasted_iota(jnp.int32, (no, 2 * no), 1)).astype(F32)
    twice = (lax.rem(lax.broadcasted_iota(jnp.int32, (no, 4 * no), 1), 2 * no)
             == lax.broadcasted_iota(jnp.int32, (no, 4 * no), 0)).astype(F32)
    u_re, u_im = prop[0], prop[1]
    u_real = jnp.concatenate(
        [exact(u_re, first) - exact(u_im, second), exact(u_im, first) + exact(u_re, second)], axis=0
    )
    u_twice = jnp.concatenate([exact(u_re, twice), exact(u_im, twice)], axis=0)
    pick = (
        lax.rem(lax.broadcasted_iota(jnp.int32, (2 * no, 128), 0), no)
        == lax.broadcasted_iota(jnp.int32, (2 * no, 128), 1)
    )

    def damping_col(d_row):
        wide = jnp.broadcast_to(d_row, (2 * no, 128))
        return jnp.sum(jnp.where(pick, wide, 0.0), axis=1, keepdims=True)

    def begin(ref, l_packed):
        a0 = damping_col(ref[0:1, :]) * u_real
        prod = mm3(split(a0[:, 0:no]), split(l_packed))
        return joined_halves(prod[0:no], prod[no:])

    def joined_halves(a, b):
        return jnp.concatenate(
            [joined(a[:, 0:cols], b[:, 0:cols]), joined(a[:, cols:], b[:, cols:])], axis=1
        )

    start = begin(dmine, jnp.concatenate([l0[0:no], l1[0:no]], axis=1))
    start = jnp.where(me_sa == 0, start, jnp.zeros_like(start))
    start = jnp.concatenate([start, jnp.zeros((rows - no, 2 * cols), F32)], axis=0)

    wait_sa(dall, s_d, r_d)
    ops = []
    for q in range(n_sa):
        d_odd = damping_col(dall[q, 1:2, :])
        even = damping_col(dall[q, 0:1, :]) * u_real
        both = exact(d_odd * u_real, even)
        ops.append((split(jnp.concatenate([even, both], axis=0)), d_odd * u_twice))

    wait_sa(hist, s_h, r_h)
    for k in range(1, n_tp):
        who = lax.rem(me_tp + k, n_tp)
        remote(spec1.at[who], spec1.at[who], s_s.at[k - 1], r_s.at[who], (me_sa, who)).wait_recv()
    history = hist[...].reshape(n_sa * rows, 2 * cols)
    acc = None
    for c in range(n_tp):
        part = mm(spec1[c], history[c * cols : (c + 1) * cols, :])
        acc = part if acc is None else acc + part
    force = scale * joined_halves(acc[0:rows], acc[rows:]) + start
    fst[0] = force[:, 0:cols].astype(BF16)
    fst[1] = force[:, cols:].astype(BF16)
    send_half(fst, fall, s_f, r_f)
    fall[me_sa] = fst[core]

    lane = lax.broadcasted_iota(jnp.int32, (4 * no, 4 * no), 1)
    line = lax.broadcasted_iota(jnp.int32, (4 * no, 4 * no), 0)
    here = jnp.where(line < 2 * no, line, line - no)
    unit_rows = jnp.logical_or(line < no, jnp.logical_and(line >= 2 * no, line < 3 * no))
    last = None
    for q in range(n_sa):
        (a_hi, a_lo), odd_cols = ops[q]
        at = (q % 2) * 2 * no
        placed = jnp.where(jnp.logical_and(unit_rows, lane == here + at), 1.0, 0.0)
        span = lax.broadcasted_iota(jnp.int32, (2 * no, 4 * no), 1)
        kept = jnp.where(jnp.logical_and(span >= at, span < at + no), odd_cols, 0.0)
        placed = placed + jnp.concatenate([jnp.zeros_like(kept), kept], axis=0)
        if q == 0:
            block = placed
        else:
            high, low = last
            wide = mm(jnp.concatenate([a_hi, a_lo], axis=0), high)
            moved = wide[0 : 4 * no] + (wide[4 * no :] + mm(a_hi, low))
            if q % 2 == 0:
                block = jnp.concatenate([moved, placed], axis=1)
            else:
                width = moved.shape[1] - 4 * no
                tail = moved[:, width:] + placed
                block = tail if width == 0 else jnp.concatenate([moved[:, 0:width], tail], axis=1)
        last = split(block[2 * no :])
        width = block.shape[1]
        pmat[q, :, 0:width] = block.astype(BF16)
        if width < n_sa * rows:
            pmat[q, :, width:] = jnp.zeros((4 * no, n_sa * rows - width), BF16)

    first_rows = hist[0, 0:no, :].astype(F32)
    q_left = pmat[me_sa][:, 0:no]
    q_own = mm(q_left, begin(dall.at[0], first_rows).astype(BF16))
    q_own = joined_halves(*split_parts(q_own, no))

    wait_sa(gall, s_g, r_g)
    wait_sa(fall, s_f, r_f)
    step = 4
    forces = fall[...].reshape(n_sa * rows, cols)
    factor8 = jnp.concatenate([factor2] * step, axis=0)
    mine = y2.at[core]
    for r in range(n_sa // step):
        depth = (r + 1) * step * rows
        left = pmat[r * step : (r + 1) * step, :, 0:depth].reshape(step * 2 * rows, depth)
        x = joined(*split_parts(mm(left, forces[0:depth]), no))
        mine[r * step : (r + 1) * step] = x.astype(BF16).reshape(step, rows, cols)
        g = gall[r * step : (r + 1) * step].reshape(step * rows, cols).astype(F32)
        s2[r * step * rows : (r + 1) * step * rows, :] = spectral_packed(x, g, factor8).astype(BF16)
    left = pmat[pl.ds(2 * pair, 2)].reshape(4 * rows, n_sa * rows)
    moved = joined(*split_parts(mm(left, s2[...]), no)).astype(BF16)
    pst[0] = moved[0:rows]
    pst[1] = moved[rows:]
    for k in range(1, n_tp):
        who = lax.rem(me_tp + k, n_tp)
        push(pst.at[core], ps.at[2 * me_tp + core], s_p.at[k - 1], r_p.at[2 * me_tp + core], (me_sa, who))
        push(pst.at[1 - core], ps.at[2 * me_tp + core], s_q.at[k - 1], r_p.at[2 * me_tp + core], (sib, who))
    push(y2.at[core], y2.at[core], s_y.at[0], r_y.at[0], (sib, me_tp))
    push(pst.at[1 - core], ps.at[2 * me_tp + core], s_q.at[n_tp - 1], r_p.at[2 * me_tp + core], (sib, me_tp))
    ps[2 * me_tp + core] = pst[core]

    remote(y2.at[1 - core], y2.at[1 - core], s_y.at[0], r_y.at[0], (sib, me_tp)).wait_recv()
    for h in range(2):
        y = y2[h]
        turned = signed(swap(y.reshape(n_sa * rows, cols).astype(F32))).astype(BF16)
        yst[:, 0:rows, h * cols : (h + 1) * cols] = y
        yst[:, rows:, h * cols : (h + 1) * cols] = turned.reshape(n_sa, rows, cols)
    base = 0.5 * (jnp.concatenate([y2[0, me_sa], y2[1, me_sa]], axis=1).astype(F32) + q_own)

    for k in range(n_tp):
        who = lax.rem(me_tp + k, n_tp)
        for h in (core, 1 - core):
            if k == 0 and h is core:
                continue
            at = 2 * who + h
            remote(ps.at[at], ps.at[at], s_p.at[0], r_p.at[at], (me_sa, who)).wait_recv()
    left = jnp.concatenate([ps[n] for n in range(2 * n_tp)], axis=1)
    final = base + (0.5 * scale) * mm(left, yst[...].reshape(2 * n_sa * rows, 2 * cols))
    f0, f1 = final[:, 0:cols], final[:, cols:]
    low = low_lanes(f0)
    out[0] = jnp.where(low, f0, swap(f1)).reshape(win.shape[2], no, cols)
    out[1] = jnp.where(low, swap(f0), f1).reshape(win.shape[2], no, cols)
    for copy in pending:
        copy.wait_send()


def shards(window, damping, propagator, coupling):
    n_sa, n_tp = lax.axis_size("sa"), lax.axis_size("tp")
    no = coupling.shape[0]
    block = window.shape[2]
    cols = window.shape[4]
    rows = block * no
    scale = 1.0 / (block * n_sa * math.sqrt(no))
    dma = lambda n: pltpu.SemaphoreType.DMA((n,))
    vm = pl.BlockSpec(memory_space=pltpu.VMEM)
    sems = []
    for n, m in ((n_sa, n_sa), (n_sa, n_sa), (n_sa, n_sa), (n_tp, n_tp), (n_sa, n_sa),
                 (n_tp, 2 * n_tp), (n_tp, 1), (1, 1)):
        sems += [dma(n), dma(m)]
    return pl.pallas_call(
        functools.partial(kernel, n_sa, n_tp, scale),
        out_shape=pltpu.VMEM((2, block, no, cols), F32),
        in_specs=[pl.BlockSpec(memory_space=pl.ANY)] * 4,
        out_specs=vm,
        scratch_shapes=[
            pltpu.VMEM(window.shape, F32),
            pltpu.VMEM(damping.shape, F32),
            pltpu.VMEM(propagator.shape, F32),
            pltpu.VMEM((1, no), F32),
            dma(4),
            pltpu.VMEM((n_sa, 8, 128), F32),
            pltpu.VMEM((n_sa, rows, 2 * cols), BF16),
            pltpu.VMEM((n_tp, 2 * rows, cols), BF16),
            pltpu.VMEM((2, rows, cols), BF16),
            pltpu.VMEM((n_sa, rows, cols), BF16),
            pltpu.VMEM((2, rows, cols), BF16),
            pltpu.VMEM((n_sa, rows, cols), BF16),
            pltpu.VMEM((n_sa, 2 * rows, n_sa * rows), BF16),
            pltpu.VMEM((n_sa * rows, cols), BF16),
            pltpu.VMEM((2, rows, cols), BF16),
            pltpu.VMEM((2 * n_tp, rows, cols), BF16),
            pltpu.VMEM((2, n_sa, rows, cols), BF16),
            pltpu.VMEM((n_sa, 2 * rows, 2 * cols), BF16),
        ] + sems,
        compiler_params=pltpu.CompilerParams(collective_id=0, has_side_effects=True),
        name="kadanoff",
    )(window, damping, propagator, coupling.reshape(1, no))


def solution(mesh):
    return jax.shard_map(
        shards,
        mesh=mesh,
        in_specs=(P(None, None, "sa", None, "tp"), P("sa", None), P(), P()),
        out_specs=P(None, "sa", None, "tp"),
        check_vma=False,
    )
```

```python
import functools
import math

import jax
import jax.numpy as jnp
from jax import lax
from jax.experimental import pallas as pl
from jax.experimental.pallas import tpu as pltpu
from jax.sharding import PartitionSpec as P

MESH = pl.DeviceIdType.MESH
F32 = jnp.float32
BF16 = jnp.bfloat16


def exact(a, b):
    return jnp.dot(a, b, precision=lax.Precision.HIGHEST, preferred_element_type=F32)


def split(x):
    high = x.astype(BF16)
    return high, (x - high.astype(F32)).astype(BF16)


def mm(a, b):
    return jnp.dot(a, b, preferred_element_type=F32)


def mm3(a, b):
    return mm(a[0], b[0]) + (mm(a[0], b[1]) + mm(a[1], b[0]))


def spectral_of(x_re, x_im, g_re, g_im, factor):
    lsquare_re = x_re * x_re - x_im * x_im
    lsquare_im = 2.0 * x_re * x_im
    gsquare_re = g_re * g_re - g_im * g_im
    gsquare_im = 2.0 * g_re * g_im
    sless_re = -factor * (lsquare_re * g_re + lsquare_im * g_im)
    sless_im = -factor * (lsquare_im * g_re - lsquare_re * g_im)
    sgreat_re = -factor * (gsquare_re * x_re + gsquare_im * x_im)
    sgreat_im = -factor * (gsquare_im * x_re - gsquare_re * x_im)
    return jnp.concatenate([sgreat_re - sless_re, sgreat_im - sless_im], axis=0).astype(BF16)


def low_lanes(x):
    return lax.broadcasted_iota(jnp.int32, x.shape, 1) < x.shape[1] // 2


def swap(x):
    return pltpu.roll(x, x.shape[1] // 2, 1)


def signed(x):
    return jnp.where(low_lanes(x), -x, x)


def pack(re, im):
    low = low_lanes(re)
    return jnp.where(low, re, swap(im)), jnp.where(low, swap(re), im)


def joined(a, b):
    return a + signed(swap(b))


def split_parts(x, no):
    n = x.shape[0] // (2 * no)
    y = x.reshape(n, 2, no, x.shape[1])
    return y[:, 0].reshape(n * no, x.shape[1]), y[:, 1].reshape(n * no, x.shape[1])


def spectral_packed(x, g, factor):
    low = low_lanes(x)
    xs, gs = swap(x), swap(g)
    x_re, x_im = jnp.where(low, x, xs), jnp.where(low, xs, x)
    g_re, g_im = jnp.where(low, g, gs), jnp.where(low, gs, g)
    z = x * g_re - signed(xs * g_im)
    return factor * (z * (x_re + signed(g_re)) + swap(z) * (signed(x_im) - g_im))


def kernel(
    n_sa, n_tp, scale,
    win_in, damp_in, prop_in, coup_in, out,
    win, damp, prop, coup, s_in, dall, hist, spec1, gst, gall, fst, fall, pmat, s2, pst, ps, y2, yst,
    s_d, r_d, s_h, r_h, s_k, r_k, s_g, r_g, s_s, r_s, s_f, r_f, s_p, r_p, s_q, r_q, s_y, r_y,
):
    me_sa = lax.axis_index("sa")
    me_tp = lax.axis_index("tp")
    no = prop.shape[1]
    cols = win.shape[4]
    rows = win.shape[2] * no
    core = lax.rem(me_sa, 2)
    pair = lax.div(me_sa, 2)
    sib = pair * 2 + 1 - core

    barrier = pltpu.get_barrier_semaphore()
    for k in range(1, n_tp):
        who = lax.rem(me_tp + k, n_tp)
        pl.semaphore_signal(barrier, inc=1, device_id=(me_sa, who), device_id_type=MESH)
        pl.semaphore_signal(barrier, inc=1, device_id=(sib, who), device_id_type=MESH)
    for k in range(1, n_sa):
        pl.semaphore_signal(
            barrier, inc=1, device_id=(lax.rem(me_sa + k, n_sa), me_tp), device_id_type=MESH
        )

    loads = [
        pltpu.make_async_copy(src, dst, s_in.at[n])
        for n, (src, dst) in enumerate(
            [(win_in, win), (coup_in, coup), (damp_in, damp), (prop_in, prop)]
        )
    ]
    for load in loads:
        load.start()

    pending = []

    def remote(src, dst, send, recv, dev):
        return pltpu.make_async_remote_copy(
            src_ref=src, dst_ref=dst, send_sem=send, recv_sem=recv,
            device_id=dev, device_id_type=MESH,
        )

    def push(src, dst, send, recv, dev):
        copy = remote(src, dst, send, recv, dev)
        copy.start()
        pending.append(copy)

    def send_sa(buf, send, recv):
        for k in range(1, n_sa):
            who = lax.rem(me_sa + k, n_sa)
            push(buf.at[me_sa], buf.at[me_sa], send.at[k - 1], recv.at[me_sa], (who, me_tp))

    def send_half(src, buf, send, recv):
        for k in range(1, n_sa):
            who = lax.rem(me_sa + k, n_sa)
            push(src.at[lax.rem(who, 2)], buf.at[me_sa], send.at[k - 1], recv.at[me_sa], (who, me_tp))

    def hand_on(source, n):
        half = hist.at[core, source]
        push(half, half, s_k.at[n], r_k.at[source], (sib, me_tp))

    def abroad():
        for k in range(1, n_sa // 2):
            other = lax.rem(pair + k, n_sa // 2) * 2
            yield other + core
            yield other + 1 - core

    def wait_sa(buf, send, recv):
        for k in range(1, n_sa):
            who = lax.rem(me_sa + k, n_sa)
            remote(buf.at[who], buf.at[who], send.at[k - 1], recv.at[who], (who, me_tp)).wait_recv()

    for load in loads:
        load.wait()

    row_id = lax.broadcasted_iota(jnp.int32, (no, cols), 0)
    lane_id = lax.broadcasted_iota(jnp.int32, (no, cols), 1)
    tiled = (lax.rem(lane_id, no) == row_id).astype(F32)
    c_row = coup[...]
    c_lanes = exact(c_row, tiled)
    eye = lax.broadcasted_iota(jnp.int32, (no, no), 0) == lax.broadcasted_iota(jnp.int32, (no, no), 1)
    c_col = jnp.sum(jnp.where(eye, jnp.broadcast_to(c_row, (no, no)), 0.0), axis=1, keepdims=True)
    factor = c_col * c_lanes
    factor2 = jnp.concatenate([factor] * win.shape[2], axis=0)

    l_re = win[0, 0].reshape(rows, cols)
    l_im = win[0, 1].reshape(rows, cols)
    g_re = win[1, 0].reshape(rows, cols)
    g_im = win[1, 1].reshape(rows, cols)
    spec1[me_tp] = spectral_of(l_re, l_im, g_re, g_im, factor2)
    l0, l1 = pack(l_re, l_im)
    hist[0, me_sa] = l0.astype(BF16)
    hist[1, me_sa] = l1.astype(BF16)
    dmine = dall.at[me_sa]
    dmine[...] = jnp.zeros(dmine.shape, F32)
    dmine[0:2, 0:no] = damp[...]
    g0, g1 = pack(g_re, g_im)
    gst[0] = g0.astype(BF16)
    gst[1] = g1.astype(BF16)
    gall[me_sa] = gst[core]

    pl.semaphore_wait(barrier, n_sa - 1 + 2 * (n_tp - 1))
    for k in range(1, n_tp):
        who = lax.rem(me_tp + k, n_tp)
        push(spec1.at[me_tp], spec1.at[me_tp], s_s.at[k - 1], r_s.at[me_tp], (me_sa, who))
    for k in range(1, n_sa):
        who = lax.rem(me_sa + k, n_sa)
        half = hist.at[lax.rem(who, 2), me_sa]
        push(half, half, s_h.at[k - 1], r_h.at[me_sa], (who, me_tp))
    hand_on(me_sa, 0)
    send_sa(dall, s_d, r_d)
    send_half(gst, gall, s_g, r_g)

    first = (lax.broadcasted_iota(jnp.int32, (no, 2 * no), 0)
             == lax.broadcasted_iota(jnp.int32, (no, 2 * no), 1)).astype(F32)
    second = (lax.broadcasted_iota(jnp.int32, (no, 2 * no), 0) + no
              == lax.broadcasted_iota(jnp.int32, (no, 2 * no), 1)).astype(F32)
    twice = (lax.rem(lax.broadcasted_iota(jnp.int32, (no, 4 * no), 1), 2 * no)
             == lax.broadcasted_iota(jnp.int32, (no, 4 * no), 0)).astype(F32)
    u_re, u_im = prop[0], prop[1]
    u_real = jnp.concatenate(
        [exact(u_re, first) - exact(u_im, second), exact(u_im, first) + exact(u_re, second)], axis=0
    )
    u_twice = jnp.concatenate([exact(u_re, twice), exact(u_im, twice)], axis=0)
    pick = (
        lax.rem(lax.broadcasted_iota(jnp.int32, (2 * no, 128), 0), no)
        == lax.broadcasted_iota(jnp.int32, (2 * no, 128), 1)
    )

    def damping_col(d_row):
        wide = jnp.broadcast_to(d_row, (2 * no, 128))
        return jnp.sum(jnp.where(pick, wide, 0.0), axis=1, keepdims=True)

    def begin(ref, l_packed):
        a0 = damping_col(ref[0:1, :]) * u_real
        prod = mm3(split(a0[:, 0:no]), split(l_packed))
        return joined_halves(prod[0:no], prod[no:])

    def joined_halves(a, b):
        return jnp.concatenate(
            [joined(a[:, 0:cols], b[:, 0:cols]), joined(a[:, cols:], b[:, cols:])], axis=1
        )

    start = begin(dmine, jnp.concatenate([l0[0:no], l1[0:no]], axis=1))
    start = jnp.where(me_sa == 0, start, jnp.zeros_like(start))
    start = jnp.concatenate([start, jnp.zeros((rows - no, 2 * cols), F32)], axis=0)

    wait_sa(dall, s_d, r_d)
    ops = []
    for q in range(n_sa):
        d_odd = damping_col(dall[q, 1:2, :])
        even = damping_col(dall[q, 0:1, :]) * u_real
        both = exact(d_odd * u_real, even)
        ops.append((split(jnp.concatenate([even, both], axis=0)), d_odd * u_twice))

    for n, who in enumerate(abroad()):
        half = hist.at[core, who]
        remote(half, half, s_h.at[0], r_h.at[who], (who, me_tp)).wait_recv()
        hand_on(who, n + 1)
    half = hist.at[core, sib]
    remote(half, half, s_h.at[0], r_h.at[sib], (sib, me_tp)).wait_recv()
    half = hist.at[1 - core, sib]
    remote(half, half, s_k.at[0], r_k.at[sib], (sib, me_tp)).wait_recv()
    for who in abroad():
        half = hist.at[1 - core, who]
        remote(half, half, s_k.at[0], r_k.at[who], (sib, me_tp)).wait_recv()
    for k in range(1, n_tp):
        who = lax.rem(me_tp + k, n_tp)
        remote(spec1.at[who], spec1.at[who], s_s.at[k - 1], r_s.at[who], (me_sa, who)).wait_recv()
    history = jnp.concatenate([hist[h].reshape(n_sa * rows, cols) for h in range(2)], axis=1)
    acc = None
    for c in range(n_tp):
        part = mm(spec1[c], history[c * cols : (c + 1) * cols, :])
        acc = part if acc is None else acc + part
    force = scale * joined_halves(acc[0:rows], acc[rows:]) + start
    fst[0] = force[:, 0:cols].astype(BF16)
    fst[1] = force[:, cols:].astype(BF16)
    send_half(fst, fall, s_f, r_f)
    fall[me_sa] = fst[core]

    lane = lax.broadcasted_iota(jnp.int32, (4 * no, 4 * no), 1)
    line = lax.broadcasted_iota(jnp.int32, (4 * no, 4 * no), 0)
    here = jnp.where(line < 2 * no, line, line - no)
    unit_rows = jnp.logical_or(line < no, jnp.logical_and(line >= 2 * no, line < 3 * no))
    last = None
    for q in range(n_sa):
        (a_hi, a_lo), odd_cols = ops[q]
        at = (q % 2) * 2 * no
        placed = jnp.where(jnp.logical_and(unit_rows, lane == here + at), 1.0, 0.0)
        span = lax.broadcasted_iota(jnp.int32, (2 * no, 4 * no), 1)
        kept = jnp.where(jnp.logical_and(span >= at, span < at + no), odd_cols, 0.0)
        placed = placed + jnp.concatenate([jnp.zeros_like(kept), kept], axis=0)
        if q == 0:
            block = placed
        else:
            high, low = last
            wide = mm(jnp.concatenate([a_hi, a_lo], axis=0), high)
            moved = wide[0 : 4 * no] + (wide[4 * no :] + mm(a_hi, low))
            if q % 2 == 0:
                block = jnp.concatenate([moved, placed], axis=1)
            else:
                width = moved.shape[1] - 4 * no
                tail = moved[:, width:] + placed
                block = tail if width == 0 else jnp.concatenate([moved[:, 0:width], tail], axis=1)
        last = split(block[2 * no :])
        width = block.shape[1]
        pmat[q, :, 0:width] = block.astype(BF16)
        if width < n_sa * rows:
            pmat[q, :, width:] = jnp.zeros((4 * no, n_sa * rows - width), BF16)

    first_rows = jnp.concatenate([hist[h, 0, 0:no] for h in range(2)], axis=1).astype(F32)
    q_left = pmat[me_sa][:, 0:no]
    q_own = mm(q_left, begin(dall.at[0], first_rows).astype(BF16))
    q_own = joined_halves(*split_parts(q_own, no))

    wait_sa(gall, s_g, r_g)
    wait_sa(fall, s_f, r_f)
    step = 4
    forces = fall[...].reshape(n_sa * rows, cols)
    factor8 = jnp.concatenate([factor2] * step, axis=0)
    mine = y2.at[core]
    for r in range(n_sa // step):
        depth = (r + 1) * step * rows
        left = pmat[r * step : (r + 1) * step, :, 0:depth].reshape(step * 2 * rows, depth)
        x = joined(*split_parts(mm(left, forces[0:depth]), no))
        mine[r * step : (r + 1) * step] = x.astype(BF16).reshape(step, rows, cols)
        g = gall[r * step : (r + 1) * step].reshape(step * rows, cols).astype(F32)
        s2[r * step * rows : (r + 1) * step * rows, :] = spectral_packed(x, g, factor8).astype(BF16)
    left = pmat[pl.ds(2 * pair, 2)].reshape(4 * rows, n_sa * rows)
    moved = joined(*split_parts(mm(left, s2[...]), no)).astype(BF16)
    pst[0] = moved[0:rows]
    pst[1] = moved[rows:]
    for k in range(1, n_tp):
        who = lax.rem(me_tp + k, n_tp)
        push(pst.at[core], ps.at[2 * me_tp + core], s_p.at[k - 1], r_p.at[2 * me_tp + core], (me_sa, who))
        push(pst.at[1 - core], ps.at[2 * me_tp + core], s_q.at[k - 1], r_p.at[2 * me_tp + core], (sib, who))
    push(y2.at[core], y2.at[core], s_y.at[0], r_y.at[0], (sib, me_tp))
    push(pst.at[1 - core], ps.at[2 * me_tp + core], s_q.at[n_tp - 1], r_p.at[2 * me_tp + core], (sib, me_tp))
    ps[2 * me_tp + core] = pst[core]

    remote(y2.at[1 - core], y2.at[1 - core], s_y.at[0], r_y.at[0], (sib, me_tp)).wait_recv()
    for h in range(2):
        y = y2[h]
        turned = signed(swap(y.reshape(n_sa * rows, cols).astype(F32))).astype(BF16)
        yst[:, 0:rows, h * cols : (h + 1) * cols] = y
        yst[:, rows:, h * cols : (h + 1) * cols] = turned.reshape(n_sa, rows, cols)
    base = 0.5 * (jnp.concatenate([y2[0, me_sa], y2[1, me_sa]], axis=1).astype(F32) + q_own)

    for k in range(n_tp):
        who = lax.rem(me_tp + k, n_tp)
        for h in (core, 1 - core):
            if k == 0 and h is core:
                continue
            at = 2 * who + h
            remote(ps.at[at], ps.at[at], s_p.at[0], r_p.at[at], (me_sa, who)).wait_recv()
    left = jnp.concatenate([ps[n] for n in range(2 * n_tp)], axis=1)
    final = base + (0.5 * scale) * mm(left, yst[...].reshape(2 * n_sa * rows, 2 * cols))
    f0, f1 = final[:, 0:cols], final[:, cols:]
    low = low_lanes(f0)
    out[0] = jnp.where(low, f0, swap(f1)).reshape(win.shape[2], no, cols)
    out[1] = jnp.where(low, swap(f0), f1).reshape(win.shape[2], no, cols)
    for copy in pending:
        copy.wait_send()


def shards(window, damping, propagator, coupling):
    n_sa, n_tp = lax.axis_size("sa"), lax.axis_size("tp")
    no = coupling.shape[0]
    block = window.shape[2]
    cols = window.shape[4]
    rows = block * no
    scale = 1.0 / (block * n_sa * math.sqrt(no))
    dma = lambda n: pltpu.SemaphoreType.DMA((n,))
    vm = pl.BlockSpec(memory_space=pltpu.VMEM)
    sems = []
    for n, m in ((n_sa, n_sa), (n_sa, n_sa), (n_sa, n_sa), (n_sa, n_sa), (n_tp, n_tp), (n_sa, n_sa),
                 (n_tp, 2 * n_tp), (n_tp, 1), (1, 1)):
        sems += [dma(n), dma(m)]
    return pl.pallas_call(
        functools.partial(kernel, n_sa, n_tp, scale),
        out_shape=pltpu.VMEM((2, block, no, cols), F32),
        in_specs=[pl.BlockSpec(memory_space=pl.ANY)] * 4,
        out_specs=vm,
        scratch_shapes=[
            pltpu.VMEM(window.shape, F32),
            pltpu.VMEM(damping.shape, F32),
            pltpu.VMEM(propagator.shape, F32),
            pltpu.VMEM((1, no), F32),
            dma(4),
            pltpu.VMEM((n_sa, 8, 128), F32),
            pltpu.VMEM((2, n_sa, rows, cols), BF16),
            pltpu.VMEM((n_tp, 2 * rows, cols), BF16),
            pltpu.VMEM((2, rows, cols), BF16),
            pltpu.VMEM((n_sa, rows, cols), BF16),
            pltpu.VMEM((2, rows, cols), BF16),
            pltpu.VMEM((n_sa, rows, cols), BF16),
            pltpu.VMEM((n_sa, 2 * rows, n_sa * rows), BF16),
            pltpu.VMEM((n_sa * rows, cols), BF16),
            pltpu.VMEM((2, rows, cols), BF16),
            pltpu.VMEM((2 * n_tp, rows, cols), BF16),
            pltpu.VMEM((2, n_sa, rows, cols), BF16),
            pltpu.VMEM((n_sa, 2 * rows, 2 * cols), BF16),
        ] + sems,
        compiler_params=pltpu.CompilerParams(collective_id=0, has_side_effects=True),
        name="kadanoff",
    )(window, damping, propagator, coupling.reshape(1, no))


def solution(mesh):
    return jax.shard_map(
        shards,
        mesh=mesh,
        in_specs=(P(None, None, "sa", None, "tp"), P("sa", None), P(), P()),
        out_specs=P(None, "sa", None, "tp"),
        check_vma=False,
    )
```

```python
import functools
import math

import jax
import jax.numpy as jnp
from jax import lax
from jax.experimental import pallas as pl
from jax.experimental.pallas import tpu as pltpu
from jax.sharding import PartitionSpec as P

MESH = pl.DeviceIdType.MESH
F32 = jnp.float32
BF16 = jnp.bfloat16


def exact(a, b):
    return jnp.dot(a, b, precision=lax.Precision.HIGHEST, preferred_element_type=F32)


def split(x):
    high = x.astype(BF16)
    return high, (x - high.astype(F32)).astype(BF16)


def mm(a, b):
    return jnp.dot(a, b, preferred_element_type=F32)


def mm3(a, b):
    return mm(a[0], b[0]) + (mm(a[0], b[1]) + mm(a[1], b[0]))


def spectral_of(x_re, x_im, g_re, g_im, factor):
    lsquare_re = x_re * x_re - x_im * x_im
    lsquare_im = 2.0 * x_re * x_im
    gsquare_re = g_re * g_re - g_im * g_im
    gsquare_im = 2.0 * g_re * g_im
    sless_re = -factor * (lsquare_re * g_re + lsquare_im * g_im)
    sless_im = -factor * (lsquare_im * g_re - lsquare_re * g_im)
    sgreat_re = -factor * (gsquare_re * x_re + gsquare_im * x_im)
    sgreat_im = -factor * (gsquare_im * x_re - gsquare_re * x_im)
    return jnp.concatenate([sgreat_re - sless_re, sgreat_im - sless_im], axis=0).astype(BF16)


def low_lanes(x):
    return lax.broadcasted_iota(jnp.int32, x.shape, 1) < x.shape[1] // 2


def swap(x):
    return pltpu.roll(x, x.shape[1] // 2, 1)


def signed(x):
    return jnp.where(low_lanes(x), -x, x)


def pack(re, im):
    low = low_lanes(re)
    return jnp.where(low, re, swap(im)), jnp.where(low, swap(re), im)


def joined(a, b):
    return a + signed(swap(b))


def split_parts(x, no):
    n = x.shape[0] // (2 * no)
    y = x.reshape(n, 2, no, x.shape[1])
    return y[:, 0].reshape(n * no, x.shape[1]), y[:, 1].reshape(n * no, x.shape[1])


def spectral_packed(x, g, factor):
    low = low_lanes(x)
    xs, gs = swap(x), swap(g)
    x_re, x_im = jnp.where(low, x, xs), jnp.where(low, xs, x)
    g_re, g_im = jnp.where(low, g, gs), jnp.where(low, gs, g)
    z = x * g_re - signed(xs * g_im)
    return factor * (z * (x_re + signed(g_re)) + swap(z) * (signed(x_im) - g_im))


def kernel(
    n_sa, n_tp, scale,
    win_in, damp_in, prop_in, coup_in, out,
    win, damp, prop, coup, s_in, dall, hist, spec1, gst, gall, fst, fall, pmat, s2, pst, ps, y2, yst,
    s_d, r_d, s_h, r_h, s_k, r_k, s_g, r_g, s_s, r_s, s_f, r_f, s_p, r_p, s_q, r_q, s_y, r_y,
):
    me_sa = lax.axis_index("sa")
    me_tp = lax.axis_index("tp")
    no = prop.shape[1]
    cols = win.shape[4]
    rows = win.shape[2] * no
    core = lax.rem(me_sa, 2)
    pair = lax.div(me_sa, 2)
    sib = pair * 2 + 1 - core

    barrier = pltpu.get_barrier_semaphore()
    for k in range(1, n_tp):
        who = lax.rem(me_tp + k, n_tp)
        pl.semaphore_signal(barrier, inc=1, device_id=(me_sa, who), device_id_type=MESH)
        pl.semaphore_signal(barrier, inc=1, device_id=(sib, who), device_id_type=MESH)
    for k in range(1, n_sa):
        pl.semaphore_signal(
            barrier, inc=1, device_id=(lax.rem(me_sa + k, n_sa), me_tp), device_id_type=MESH
        )

    loads = [
        pltpu.make_async_copy(src, dst, s_in.at[n])
        for n, (src, dst) in enumerate(
            [(win_in, win), (coup_in, coup), (damp_in, damp), (prop_in, prop)]
        )
    ]
    for load in loads:
        load.start()

    pending = []

    def remote(src, dst, send, recv, dev):
        return pltpu.make_async_remote_copy(
            src_ref=src, dst_ref=dst, send_sem=send, recv_sem=recv,
            device_id=dev, device_id_type=MESH,
        )

    def push(src, dst, send, recv, dev):
        copy = remote(src, dst, send, recv, dev)
        copy.start()
        pending.append(copy)

    def send_sa(buf, send, recv):
        for k in range(1, n_sa):
            who = lax.rem(me_sa + k, n_sa)
            push(buf.at[me_sa], buf.at[me_sa], send.at[k - 1], recv.at[me_sa], (who, me_tp))

    def send_half(src, buf, send, recv):
        for k in range(1, n_sa):
            who = lax.rem(me_sa + k, n_sa)
            push(src.at[lax.rem(who, 2)], buf.at[me_sa], send.at[k - 1], recv.at[me_sa], (who, me_tp))

    def hand_on(source, n):
        half = hist.at[core, source]
        push(half, half, s_k.at[n], r_k.at[source], (sib, me_tp))

    def abroad():
        for k in range(1, n_sa // 2):
            other = lax.rem(pair + k, n_sa // 2) * 2
            yield other + core
            yield other + 1 - core

    def wait_sa(buf, send, recv):
        for k in range(1, n_sa):
            who = lax.rem(me_sa + k, n_sa)
            remote(buf.at[who], buf.at[who], send.at[k - 1], recv.at[who], (who, me_tp)).wait_recv()

    for load in loads:
        load.wait()

    row_id = lax.broadcasted_iota(jnp.int32, (no, cols), 0)
    lane_id = lax.broadcasted_iota(jnp.int32, (no, cols), 1)
    tiled = (lax.rem(lane_id, no) == row_id).astype(F32)
    c_row = coup[...]
    c_lanes = exact(c_row, tiled)
    eye = lax.broadcasted_iota(jnp.int32, (no, no), 0) == lax.broadcasted_iota(jnp.int32, (no, no), 1)
    c_col = jnp.sum(jnp.where(eye, jnp.broadcast_to(c_row, (no, no)), 0.0), axis=1, keepdims=True)
    factor = c_col * c_lanes
    factor2 = jnp.concatenate([factor] * win.shape[2], axis=0)

    l_re = win[0, 0].reshape(rows, cols)
    l_im = win[0, 1].reshape(rows, cols)
    g_re = win[1, 0].reshape(rows, cols)
    g_im = win[1, 1].reshape(rows, cols)
    spec1[me_tp] = spectral_of(l_re, l_im, g_re, g_im, factor2)
    l0, l1 = pack(l_re, l_im)
    hist[0, me_sa] = l0.astype(BF16)
    hist[1, me_sa] = l1.astype(BF16)
    dmine = dall.at[me_sa]
    dmine[...] = jnp.zeros(dmine.shape, F32)
    dmine[0:2, 0:no] = damp[...]
    g0, g1 = pack(g_re, g_im)
    gst[0] = g0.astype(BF16)
    gst[1] = g1.astype(BF16)
    gall[me_sa] = gst[core]

    pl.semaphore_wait(barrier, n_sa - 1 + 2 * (n_tp - 1))
    for k in range(1, n_tp):
        who = lax.rem(me_tp + k, n_tp)
        push(spec1.at[me_tp], spec1.at[me_tp], s_s.at[k - 1], r_s.at[me_tp], (me_sa, who))
    for k in range(1, n_sa):
        who = lax.rem(me_sa + k, n_sa)
        half = hist.at[lax.rem(who, 2), me_sa]
        push(half, half, s_h.at[k - 1], r_h.at[me_sa], (who, me_tp))
    hand_on(me_sa, 0)
    send_sa(dall, s_d, r_d)
    send_half(gst, gall, s_g, r_g)

    first = (lax.broadcasted_iota(jnp.int32, (no, 2 * no), 0)
             == lax.broadcasted_iota(jnp.int32, (no, 2 * no), 1)).astype(F32)
    second = (lax.broadcasted_iota(jnp.int32, (no, 2 * no), 0) + no
              == lax.broadcasted_iota(jnp.int32, (no, 2 * no), 1)).astype(F32)
    twice = (lax.rem(lax.broadcasted_iota(jnp.int32, (no, 4 * no), 1), 2 * no)
             == lax.broadcasted_iota(jnp.int32, (no, 4 * no), 0)).astype(F32)
    u_re, u_im = prop[0], prop[1]
    u_real = jnp.concatenate(
        [exact(u_re, first) - exact(u_im, second), exact(u_im, first) + exact(u_re, second)], axis=0
    )
    u_twice = jnp.concatenate([exact(u_re, twice), exact(u_im, twice)], axis=0)
    pick = (
        lax.rem(lax.broadcasted_iota(jnp.int32, (2 * no, 128), 0), no)
        == lax.broadcasted_iota(jnp.int32, (2 * no, 128), 1)
    )

    def damping_col(d_row):
        wide = jnp.broadcast_to(d_row, (2 * no, 128))
        return jnp.sum(jnp.where(pick, wide, 0.0), axis=1, keepdims=True)

    def begin(ref, l_packed):
        a0 = damping_col(ref[0:1, :]) * u_real
        prod = mm3(split(a0[:, 0:no]), split(l_packed))
        return joined_halves(prod[0:no], prod[no:])

    def joined_halves(a, b):
        return jnp.concatenate(
            [joined(a[:, 0:cols], b[:, 0:cols]), joined(a[:, cols:], b[:, cols:])], axis=1
        )

    start = begin(dmine, jnp.concatenate([l0[0:no], l1[0:no]], axis=1))
    start = jnp.where(me_sa == 0, start, jnp.zeros_like(start))
    start = jnp.concatenate([start, jnp.zeros((rows - no, 2 * cols), F32)], axis=0)

    for n, who in enumerate(abroad()):
        half = hist.at[core, who]
        remote(half, half, s_h.at[0], r_h.at[who], (who, me_tp)).wait_recv()
        hand_on(who, n + 1)
    half = hist.at[core, sib]
    remote(half, half, s_h.at[0], r_h.at[sib], (sib, me_tp)).wait_recv()
    half = hist.at[1 - core, sib]
    remote(half, half, s_k.at[0], r_k.at[sib], (sib, me_tp)).wait_recv()
    for who in abroad():
        half = hist.at[1 - core, who]
        remote(half, half, s_k.at[0], r_k.at[who], (sib, me_tp)).wait_recv()
    for k in range(1, n_tp):
        who = lax.rem(me_tp + k, n_tp)
        remote(spec1.at[who], spec1.at[who], s_s.at[k - 1], r_s.at[who], (me_sa, who)).wait_recv()
    history = jnp.concatenate([hist[h].reshape(n_sa * rows, cols) for h in range(2)], axis=1)
    acc = None
    for c in range(n_tp):
        part = mm(spec1[c], history[c * cols : (c + 1) * cols, :])
        acc = part if acc is None else acc + part
    force = scale * joined_halves(acc[0:rows], acc[rows:]) + start
    fst[0] = force[:, 0:cols].astype(BF16)
    fst[1] = force[:, cols:].astype(BF16)
    send_half(fst, fall, s_f, r_f)
    fall[me_sa] = fst[core]

    wait_sa(dall, s_d, r_d)
    ops = []
    for q in range(n_sa):
        d_odd = damping_col(dall[q, 1:2, :])
        even = damping_col(dall[q, 0:1, :]) * u_real
        both = exact(d_odd * u_real, even)
        ops.append((split(jnp.concatenate([even, both], axis=0)), d_odd * u_twice))

    lane = lax.broadcasted_iota(jnp.int32, (4 * no, 4 * no), 1)
    line = lax.broadcasted_iota(jnp.int32, (4 * no, 4 * no), 0)
    here = jnp.where(line < 2 * no, line, line - no)
    unit_rows = jnp.logical_or(line < no, jnp.logical_and(line >= 2 * no, line < 3 * no))
    last = None
    for q in range(n_sa):
        (a_hi, a_lo), odd_cols = ops[q]
        at = (q % 2) * 2 * no
        placed = jnp.where(jnp.logical_and(unit_rows, lane == here + at), 1.0, 0.0)
        span = lax.broadcasted_iota(jnp.int32, (2 * no, 4 * no), 1)
        kept = jnp.where(jnp.logical_and(span >= at, span < at + no), odd_cols, 0.0)
        placed = placed + jnp.concatenate([jnp.zeros_like(kept), kept], axis=0)
        if q == 0:
            block = placed
        else:
            high, low = last
            wide = mm(jnp.concatenate([a_hi, a_lo], axis=0), high)
            moved = wide[0 : 4 * no] + (wide[4 * no :] + mm(a_hi, low))
            if q % 2 == 0:
                block = jnp.concatenate([moved, placed], axis=1)
            else:
                width = moved.shape[1] - 4 * no
                tail = moved[:, width:] + placed
                block = tail if width == 0 else jnp.concatenate([moved[:, 0:width], tail], axis=1)
        last = split(block[2 * no :])
        width = block.shape[1]
        pmat[q, :, 0:width] = block.astype(BF16)
        if width < n_sa * rows:
            pmat[q, :, width:] = jnp.zeros((4 * no, n_sa * rows - width), BF16)

    first_rows = jnp.concatenate([hist[h, 0, 0:no] for h in range(2)], axis=1).astype(F32)
    q_left = pmat[me_sa][:, 0:no]
    q_own = mm(q_left, begin(dall.at[0], first_rows).astype(BF16))
    q_own = joined_halves(*split_parts(q_own, no))

    wait_sa(gall, s_g, r_g)
    wait_sa(fall, s_f, r_f)
    step = 4
    forces = fall[...].reshape(n_sa * rows, cols)
    factor8 = jnp.concatenate([factor2] * step, axis=0)
    mine = y2.at[core]
    for r in range(n_sa // step):
        depth = (r + 1) * step * rows
        left = pmat[r * step : (r + 1) * step, :, 0:depth].reshape(step * 2 * rows, depth)
        x = joined(*split_parts(mm(left, forces[0:depth]), no))
        mine[r * step : (r + 1) * step] = x.astype(BF16).reshape(step, rows, cols)
        g = gall[r * step : (r + 1) * step].reshape(step * rows, cols).astype(F32)
        s2[r * step * rows : (r + 1) * step * rows, :] = spectral_packed(x, g, factor8).astype(BF16)
    left = pmat[pl.ds(2 * pair, 2)].reshape(4 * rows, n_sa * rows)
    moved = joined(*split_parts(mm(left, s2[...]), no)).astype(BF16)
    pst[0] = moved[0:rows]
    pst[1] = moved[rows:]
    for k in range(1, n_tp):
        who = lax.rem(me_tp + k, n_tp)
        push(pst.at[core], ps.at[2 * me_tp + core], s_p.at[k - 1], r_p.at[2 * me_tp + core], (me_sa, who))
        push(pst.at[1 - core], ps.at[2 * me_tp + core], s_q.at[k - 1], r_p.at[2 * me_tp + core], (sib, who))
    push(y2.at[core], y2.at[core], s_y.at[0], r_y.at[0], (sib, me_tp))
    push(pst.at[1 - core], ps.at[2 * me_tp + core], s_q.at[n_tp - 1], r_p.at[2 * me_tp + core], (sib, me_tp))
    ps[2 * me_tp + core] = pst[core]

    remote(y2.at[1 - core], y2.at[1 - core], s_y.at[0], r_y.at[0], (sib, me_tp)).wait_recv()
    for h in range(2):
        y = y2[h]
        turned = signed(swap(y.reshape(n_sa * rows, cols).astype(F32))).astype(BF16)
        yst[:, 0:rows, h * cols : (h + 1) * cols] = y
        yst[:, rows:, h * cols : (h + 1) * cols] = turned.reshape(n_sa, rows, cols)
    base = 0.5 * (jnp.concatenate([y2[0, me_sa], y2[1, me_sa]], axis=1).astype(F32) + q_own)

    for k in range(n_tp):
        who = lax.rem(me_tp + k, n_tp)
        for h in (core, 1 - core):
            if k == 0 and h is core:
                continue
            at = 2 * who + h
            remote(ps.at[at], ps.at[at], s_p.at[0], r_p.at[at], (me_sa, who)).wait_recv()
    left = jnp.concatenate([ps[n] for n in range(2 * n_tp)], axis=1)
    final = base + (0.5 * scale) * mm(left, yst[...].reshape(2 * n_sa * rows, 2 * cols))
    f0, f1 = final[:, 0:cols], final[:, cols:]
    low = low_lanes(f0)
    out[0] = jnp.where(low, f0, swap(f1)).reshape(win.shape[2], no, cols)
    out[1] = jnp.where(low, swap(f0), f1).reshape(win.shape[2], no, cols)
    for copy in pending:
        copy.wait_send()


def shards(window, damping, propagator, coupling):
    n_sa, n_tp = lax.axis_size("sa"), lax.axis_size("tp")
    no = coupling.shape[0]
    block = window.shape[2]
    cols = window.shape[4]
    rows = block * no
    scale = 1.0 / (block * n_sa * math.sqrt(no))
    dma = lambda n: pltpu.SemaphoreType.DMA((n,))
    vm = pl.BlockSpec(memory_space=pltpu.VMEM)
    sems = []
    for n, m in ((n_sa, n_sa), (n_sa, n_sa), (n_sa, n_sa), (n_sa, n_sa), (n_tp, n_tp), (n_sa, n_sa),
                 (n_tp, 2 * n_tp), (n_tp, 1), (1, 1)):
        sems += [dma(n), dma(m)]
    return pl.pallas_call(
        functools.partial(kernel, n_sa, n_tp, scale),
        out_shape=pltpu.VMEM((2, block, no, cols), F32),
        in_specs=[pl.BlockSpec(memory_space=pl.ANY)] * 4,
        out_specs=vm,
        scratch_shapes=[
            pltpu.VMEM(window.shape, F32),
            pltpu.VMEM(damping.shape, F32),
            pltpu.VMEM(propagator.shape, F32),
            pltpu.VMEM((1, no), F32),
            dma(4),
            pltpu.VMEM((n_sa, 8, 128), F32),
            pltpu.VMEM((2, n_sa, rows, cols), BF16),
            pltpu.VMEM((n_tp, 2 * rows, cols), BF16),
            pltpu.VMEM((2, rows, cols), BF16),
            pltpu.VMEM((n_sa, rows, cols), BF16),
            pltpu.VMEM((2, rows, cols), BF16),
            pltpu.VMEM((n_sa, rows, cols), BF16),
            pltpu.VMEM((n_sa, 2 * rows, n_sa * rows), BF16),
            pltpu.VMEM((n_sa * rows, cols), BF16),
            pltpu.VMEM((2, rows, cols), BF16),
            pltpu.VMEM((2 * n_tp, rows, cols), BF16),
            pltpu.VMEM((2, n_sa, rows, cols), BF16),
            pltpu.VMEM((n_sa, 2 * rows, 2 * cols), BF16),
        ] + sems,
        compiler_params=pltpu.CompilerParams(collective_id=0, has_side_effects=True),
        name="kadanoff",
    )(window, damping, propagator, coupling.reshape(1, no))


def solution(mesh):
    return jax.shard_map(
        shards,
        mesh=mesh,
        in_specs=(P(None, None, "sa", None, "tp"), P("sa", None), P(), P()),
        out_specs=P(None, "sa", None, "tp"),
        check_vma=False,
    )
```

```python
import functools
import math

import jax
import jax.numpy as jnp
from jax import lax
from jax.experimental import pallas as pl
from jax.experimental.pallas import tpu as pltpu
from jax.sharding import PartitionSpec as P

MESH = pl.DeviceIdType.MESH
F32 = jnp.float32
BF16 = jnp.bfloat16


def exact(a, b):
    return jnp.dot(a, b, precision=lax.Precision.HIGHEST, preferred_element_type=F32)


def split(x):
    high = x.astype(BF16)
    return high, (x - high.astype(F32)).astype(BF16)


def mm(a, b):
    return jnp.dot(a, b, preferred_element_type=F32)


def mm3(a, b):
    return mm(a[0], b[0]) + (mm(a[0], b[1]) + mm(a[1], b[0]))


def spectral_of(x_re, x_im, g_re, g_im, factor):
    lsquare_re = x_re * x_re - x_im * x_im
    lsquare_im = 2.0 * x_re * x_im
    gsquare_re = g_re * g_re - g_im * g_im
    gsquare_im = 2.0 * g_re * g_im
    sless_re = -factor * (lsquare_re * g_re + lsquare_im * g_im)
    sless_im = -factor * (lsquare_im * g_re - lsquare_re * g_im)
    sgreat_re = -factor * (gsquare_re * x_re + gsquare_im * x_im)
    sgreat_im = -factor * (gsquare_im * x_re - gsquare_re * x_im)
    return jnp.concatenate([sgreat_re - sless_re, sgreat_im - sless_im], axis=0).astype(BF16)


def low_lanes(x):
    return lax.broadcasted_iota(jnp.int32, x.shape, 1) < x.shape[1] // 2


def swap(x):
    return pltpu.roll(x, x.shape[1] // 2, 1)


def signed(x):
    return jnp.where(low_lanes(x), -x, x)


def pack(re, im):
    low = low_lanes(re)
    return jnp.where(low, re, swap(im)), jnp.where(low, swap(re), im)


def joined(a, b):
    return a + signed(swap(b))


def split_parts(x, no):
    n = x.shape[0] // (2 * no)
    y = x.reshape(n, 2, no, x.shape[1])
    return y[:, 0].reshape(n * no, x.shape[1]), y[:, 1].reshape(n * no, x.shape[1])


def spectral_packed(x, g, factor):
    low = low_lanes(x)
    xs, gs = swap(x), swap(g)
    x_re, x_im = jnp.where(low, x, xs), jnp.where(low, xs, x)
    g_re, g_im = jnp.where(low, g, gs), jnp.where(low, gs, g)
    z = x * g_re - signed(xs * g_im)
    return factor * (z * (x_re + signed(g_re)) + swap(z) * (signed(x_im) - g_im))


def kernel(
    n_sa, n_tp, scale,
    win_in, damp_in, prop_in, coup_in, out,
    win, damp, prop, coup, s_in, dall, hist, spec1, gst, gall, fst, fall, pmat, s2, pst, ps, y2, yst,
    s_d, r_d, s_h, r_h, s_k, r_k, s_g, r_g, s_s, r_s, s_f, r_f, s_p, r_p, s_q, r_q, s_y, r_y,
):
    me_sa = lax.axis_index("sa")
    me_tp = lax.axis_index("tp")
    no = prop.shape[1]
    cols = win.shape[4]
    rows = win.shape[2] * no
    core = lax.rem(me_sa, 2)
    pair = lax.div(me_sa, 2)
    sib = pair * 2 + 1 - core

    barrier = pltpu.get_barrier_semaphore()
    for k in range(1, n_tp):
        who = lax.rem(me_tp + k, n_tp)
        pl.semaphore_signal(barrier, inc=1, device_id=(me_sa, who), device_id_type=MESH)
        pl.semaphore_signal(barrier, inc=1, device_id=(sib, who), device_id_type=MESH)
    for k in range(1, n_sa):
        pl.semaphore_signal(
            barrier, inc=1, device_id=(lax.rem(me_sa + k, n_sa), me_tp), device_id_type=MESH
        )

    loads = [
        pltpu.make_async_copy(src, dst, s_in.at[n])
        for n, (src, dst) in enumerate(
            [(win_in, win), (coup_in, coup), (damp_in, damp), (prop_in, prop)]
        )
    ]
    for load in loads:
        load.start()

    pending = []

    def remote(src, dst, send, recv, dev):
        return pltpu.make_async_remote_copy(
            src_ref=src, dst_ref=dst, send_sem=send, recv_sem=recv,
            device_id=dev, device_id_type=MESH,
        )

    def push(src, dst, send, recv, dev):
        copy = remote(src, dst, send, recv, dev)
        copy.start()
        pending.append(copy)

    def send_sa(buf, send, recv):
        for k in range(1, n_sa):
            who = lax.rem(me_sa + k, n_sa)
            push(buf.at[me_sa], buf.at[me_sa], send.at[k - 1], recv.at[me_sa], (who, me_tp))

    def send_half(src, buf, send, recv):
        for k in range(1, n_sa):
            who = lax.rem(me_sa + k, n_sa)
            push(src.at[lax.rem(who, 2)], buf.at[me_sa], send.at[k - 1], recv.at[me_sa], (who, me_tp))

    def hand_on(source, n):
        half = hist.at[core, source]
        push(half, half, s_k.at[n], r_k.at[source], (sib, me_tp))

    def abroad():
        for k in range(1, n_sa // 2):
            other = lax.rem(pair + k, n_sa // 2) * 2
            yield other + core
            yield other + 1 - core

    def wait_sa(buf, send, recv):
        for k in range(1, n_sa):
            who = lax.rem(me_sa + k, n_sa)
            remote(buf.at[who], buf.at[who], send.at[k - 1], recv.at[who], (who, me_tp)).wait_recv()

    for load in loads:
        load.wait()

    row_id = lax.broadcasted_iota(jnp.int32, (no, cols), 0)
    lane_id = lax.broadcasted_iota(jnp.int32, (no, cols), 1)
    tiled = (lax.rem(lane_id, no) == row_id).astype(F32)
    c_row = coup[...]
    c_lanes = exact(c_row, tiled)
    eye = lax.broadcasted_iota(jnp.int32, (no, no), 0) == lax.broadcasted_iota(jnp.int32, (no, no), 1)
    c_col = jnp.sum(jnp.where(eye, jnp.broadcast_to(c_row, (no, no)), 0.0), axis=1, keepdims=True)
    factor = c_col * c_lanes
    factor2 = jnp.concatenate([factor] * win.shape[2], axis=0)

    l_re = win[0, 0].reshape(rows, cols)
    l_im = win[0, 1].reshape(rows, cols)
    g_re = win[1, 0].reshape(rows, cols)
    g_im = win[1, 1].reshape(rows, cols)
    spec1[me_tp] = spectral_of(l_re, l_im, g_re, g_im, factor2)
    l0, l1 = pack(l_re, l_im)
    hist[0, me_sa] = l0.astype(BF16)
    hist[1, me_sa] = l1.astype(BF16)
    dmine = dall.at[me_sa]
    dmine[...] = jnp.zeros(dmine.shape, F32)
    dmine[0:2, 0:no] = damp[...]
    g0, g1 = pack(g_re, g_im)
    gst[0] = g0.astype(BF16)
    gst[1] = g1.astype(BF16)
    gall[me_sa] = gst[core]

    pl.semaphore_wait(barrier, n_sa - 1 + 2 * (n_tp - 1))
    for k in range(1, n_tp):
        who = lax.rem(me_tp + k, n_tp)
        push(spec1.at[me_tp], spec1.at[me_tp], s_s.at[k - 1], r_s.at[me_tp], (me_sa, who))
    for k in range(1, n_sa):
        who = lax.rem(me_sa + k, n_sa)
        half = hist.at[lax.rem(who, 2), me_sa]
        push(half, half, s_h.at[k - 1], r_h.at[me_sa], (who, me_tp))
    hand_on(me_sa, 0)
    send_sa(dall, s_d, r_d)
    send_half(gst, gall, s_g, r_g)

    first = (lax.broadcasted_iota(jnp.int32, (no, 2 * no), 0)
             == lax.broadcasted_iota(jnp.int32, (no, 2 * no), 1)).astype(F32)
    second = (lax.broadcasted_iota(jnp.int32, (no, 2 * no), 0) + no
              == lax.broadcasted_iota(jnp.int32, (no, 2 * no), 1)).astype(F32)
    twice = (lax.rem(lax.broadcasted_iota(jnp.int32, (no, 4 * no), 1), 2 * no)
             == lax.broadcasted_iota(jnp.int32, (no, 4 * no), 0)).astype(F32)
    u_re, u_im = prop[0], prop[1]
    u_real = jnp.concatenate(
        [exact(u_re, first) - exact(u_im, second), exact(u_im, first) + exact(u_re, second)], axis=0
    )
    u_twice = jnp.concatenate([exact(u_re, twice), exact(u_im, twice)], axis=0)
    pick = (
        lax.rem(lax.broadcasted_iota(jnp.int32, (2 * no, 128), 0), no)
        == lax.broadcasted_iota(jnp.int32, (2 * no, 128), 1)
    )

    def damping_col(d_row):
        wide = jnp.broadcast_to(d_row, (2 * no, 128))
        return jnp.sum(jnp.where(pick, wide, 0.0), axis=1, keepdims=True)

    def begin(ref, l_packed):
        a0 = damping_col(ref[0:1, :]) * u_real
        prod = mm3(split(a0[:, 0:no]), split(l_packed))
        return joined_halves(prod[0:no], prod[no:])

    def joined_halves(a, b):
        return jnp.concatenate(
            [joined(a[:, 0:cols], b[:, 0:cols]), joined(a[:, cols:], b[:, cols:])], axis=1
        )

    start = begin(dmine, jnp.concatenate([l0[0:no], l1[0:no]], axis=1))
    start = jnp.where(me_sa == 0, start, jnp.zeros_like(start))
    start = jnp.concatenate([start, jnp.zeros((rows - no, 2 * cols), F32)], axis=0)

    for n, who in enumerate(abroad()):
        half = hist.at[core, who]
        remote(half, half, s_h.at[0], r_h.at[who], (who, me_tp)).wait_recv()
        hand_on(who, n + 1)
    half = hist.at[core, sib]
    remote(half, half, s_h.at[0], r_h.at[sib], (sib, me_tp)).wait_recv()
    half = hist.at[1 - core, sib]
    remote(half, half, s_k.at[0], r_k.at[sib], (sib, me_tp)).wait_recv()
    for who in abroad():
        half = hist.at[1 - core, who]
        remote(half, half, s_k.at[0], r_k.at[who], (sib, me_tp)).wait_recv()
    for k in range(1, n_tp):
        who = lax.rem(me_tp + k, n_tp)
        remote(spec1.at[who], spec1.at[who], s_s.at[k - 1], r_s.at[who], (me_sa, who)).wait_recv()
    history = jnp.concatenate([hist[h].reshape(n_sa * rows, cols) for h in range(2)], axis=1)
    acc = None
    for c in range(n_tp):
        part = mm(spec1[c], history[c * cols : (c + 1) * cols, :])
        acc = part if acc is None else acc + part
    force = scale * joined_halves(acc[0:rows], acc[rows:]) + start
    fst[0] = force[:, 0:cols].astype(BF16)
    fst[1] = force[:, cols:].astype(BF16)
    send_half(fst, fall, s_f, r_f)
    fall[me_sa] = fst[core]

    wait_sa(dall, s_d, r_d)
    ops = []
    for q in range(n_sa):
        d_odd = damping_col(dall[q, 1:2, :])
        even = damping_col(dall[q, 0:1, :]) * u_real
        both = exact(d_odd * u_real, even)
        ops.append((split(jnp.concatenate([even, both], axis=0)), d_odd * u_twice))

    lane = lax.broadcasted_iota(jnp.int32, (4 * no, 4 * no), 1)
    line = lax.broadcasted_iota(jnp.int32, (4 * no, 4 * no), 0)
    here = jnp.where(line < 2 * no, line, line - no)
    unit_rows = jnp.logical_or(line < no, jnp.logical_and(line >= 2 * no, line < 3 * no))
    def grow(q, last):
        (a_hi, a_lo), odd_cols = ops[q]
        at = (q % 2) * 2 * no
        placed = jnp.where(jnp.logical_and(unit_rows, lane == here + at), 1.0, 0.0)
        span = lax.broadcasted_iota(jnp.int32, (2 * no, 4 * no), 1)
        kept = jnp.where(jnp.logical_and(span >= at, span < at + no), odd_cols, 0.0)
        placed = placed + jnp.concatenate([jnp.zeros_like(kept), kept], axis=0)
        if q == 0:
            block = placed
        else:
            high, low = last
            wide = mm(jnp.concatenate([a_hi, a_lo], axis=0), high)
            moved = wide[0 : 4 * no] + (wide[4 * no :] + mm(a_hi, low))
            if q % 2 == 0:
                block = jnp.concatenate([moved, placed], axis=1)
            else:
                width = moved.shape[1] - 4 * no
                tail = moved[:, width:] + placed
                block = tail if width == 0 else jnp.concatenate([moved[:, 0:width], tail], axis=1)
        width = block.shape[1]
        pmat[q, :, 0:width] = block.astype(BF16)
        if width < n_sa * rows:
            pmat[q, :, width:] = jnp.zeros((4 * no, n_sa * rows - width), BF16)
        return split(block[2 * no :])

    last = None
    for q in range(2):
        last = grow(q, last)

    def send_moved(start):
        at = 2 * me_tp + core
        for k in range(1, n_tp):
            who = lax.rem(me_tp + k, n_tp)
            start(remote(pst.at[core], ps.at[at], s_p.at[k - 1], r_p.at[at], (me_sa, who)))
            start(remote(pst.at[1 - core], ps.at[at], s_q.at[k - 1], r_p.at[at], (sib, who)))
        start(remote(pst.at[1 - core], ps.at[at], s_q.at[n_tp - 1], r_p.at[at], (sib, me_tp)))

    def apply(left, right):
        moved = joined(*split_parts(mm(left, right), no)).astype(BF16)
        pst[0] = moved[0:rows]
        pst[1] = moved[rows:]
        send_moved(lambda copy: copy.start())
        ps[2 * me_tp + core] = pst[core]

    remote(gall.at[sib], gall.at[sib], s_g.at[0], r_g.at[sib], (sib, me_tp)).wait_recv()
    remote(fall.at[sib], fall.at[sib], s_f.at[0], r_f.at[sib], (sib, me_tp)).wait_recv()

    @pl.when(pair == 0)
    def _():
        left = pmat[0:2, :, 0 : 2 * rows].reshape(4 * rows, 2 * rows)
        x = joined(*split_parts(mm(left, fall[0:2].reshape(2 * rows, cols)), no))
        g = gall[0:2].reshape(2 * rows, cols).astype(F32)
        apply(left, spectral_packed(x, g, jnp.concatenate([factor2] * 2, axis=0)).astype(BF16))

    for q in range(2, n_sa):
        last = grow(q, last)

    first_rows = jnp.concatenate([hist[h, 0, 0:no] for h in range(2)], axis=1).astype(F32)
    q_left = pmat[me_sa][:, 0:no]
    q_own = mm(q_left, begin(dall.at[0], first_rows).astype(BF16))
    q_own = joined_halves(*split_parts(q_own, no))

    for buf, send, recv in ((gall, s_g, r_g), (fall, s_f, r_f)):
        for who in abroad():
            remote(buf.at[who], buf.at[who], send.at[0], recv.at[who], (who, me_tp)).wait_recv()
    step = 4
    forces = fall[...].reshape(n_sa * rows, cols)
    factor8 = jnp.concatenate([factor2] * step, axis=0)
    mine = y2.at[core]
    for r in range(n_sa // step):
        depth = (r + 1) * step * rows
        left = pmat[r * step : (r + 1) * step, :, 0:depth].reshape(step * 2 * rows, depth)
        x = joined(*split_parts(mm(left, forces[0:depth]), no))
        mine[r * step : (r + 1) * step] = x.astype(BF16).reshape(step, rows, cols)
        g = gall[r * step : (r + 1) * step].reshape(step * rows, cols).astype(F32)
        s2[r * step * rows : (r + 1) * step * rows, :] = spectral_packed(x, g, factor8).astype(BF16)

    @pl.when(pair != 0)
    def _():
        apply(pmat[pl.ds(2 * pair, 2)].reshape(4 * rows, n_sa * rows), s2[...])

    push(y2.at[core], y2.at[core], s_y.at[0], r_y.at[0], (sib, me_tp))

    remote(y2.at[1 - core], y2.at[1 - core], s_y.at[0], r_y.at[0], (sib, me_tp)).wait_recv()
    for h in range(2):
        y = y2[h]
        turned = signed(swap(y.reshape(n_sa * rows, cols).astype(F32))).astype(BF16)
        yst[:, 0:rows, h * cols : (h + 1) * cols] = y
        yst[:, rows:, h * cols : (h + 1) * cols] = turned.reshape(n_sa, rows, cols)
    base = 0.5 * (jnp.concatenate([y2[0, me_sa], y2[1, me_sa]], axis=1).astype(F32) + q_own)

    for k in range(n_tp):
        who = lax.rem(me_tp + k, n_tp)
        for h in (core, 1 - core):
            if k == 0 and h is core:
                continue
            at = 2 * who + h
            remote(ps.at[at], ps.at[at], s_p.at[0], r_p.at[at], (me_sa, who)).wait_recv()
    left = jnp.concatenate([ps[n] for n in range(2 * n_tp)], axis=1)
    final = base + (0.5 * scale) * mm(left, yst[...].reshape(2 * n_sa * rows, 2 * cols))
    f0, f1 = final[:, 0:cols], final[:, cols:]
    low = low_lanes(f0)
    out[0] = jnp.where(low, f0, swap(f1)).reshape(win.shape[2], no, cols)
    out[1] = jnp.where(low, swap(f0), f1).reshape(win.shape[2], no, cols)
    for copy in pending:
        copy.wait_send()
    send_moved(lambda copy: copy.wait_send())


def shards(window, damping, propagator, coupling):
    n_sa, n_tp = lax.axis_size("sa"), lax.axis_size("tp")
    no = coupling.shape[0]
    block = window.shape[2]
    cols = window.shape[4]
    rows = block * no
    scale = 1.0 / (block * n_sa * math.sqrt(no))
    dma = lambda n: pltpu.SemaphoreType.DMA((n,))
    vm = pl.BlockSpec(memory_space=pltpu.VMEM)
    sems = []
    for n, m in ((n_sa, n_sa), (n_sa, n_sa), (n_sa, n_sa), (n_sa, n_sa), (n_tp, n_tp), (n_sa, n_sa),
                 (n_tp, 2 * n_tp), (n_tp, 1), (1, 1)):
        sems += [dma(n), dma(m)]
    return pl.pallas_call(
        functools.partial(kernel, n_sa, n_tp, scale),
        out_shape=pltpu.VMEM((2, block, no, cols), F32),
        in_specs=[pl.BlockSpec(memory_space=pl.ANY)] * 4,
        out_specs=vm,
        scratch_shapes=[
            pltpu.VMEM(window.shape, F32),
            pltpu.VMEM(damping.shape, F32),
            pltpu.VMEM(propagator.shape, F32),
            pltpu.VMEM((1, no), F32),
            dma(4),
            pltpu.VMEM((n_sa, 8, 128), F32),
            pltpu.VMEM((2, n_sa, rows, cols), BF16),
            pltpu.VMEM((n_tp, 2 * rows, cols), BF16),
            pltpu.VMEM((2, rows, cols), BF16),
            pltpu.VMEM((n_sa, rows, cols), BF16),
            pltpu.VMEM((2, rows, cols), BF16),
            pltpu.VMEM((n_sa, rows, cols), BF16),
            pltpu.VMEM((n_sa, 2 * rows, n_sa * rows), BF16),
            pltpu.VMEM((n_sa * rows, cols), BF16),
            pltpu.VMEM((2, rows, cols), BF16),
            pltpu.VMEM((2 * n_tp, rows, cols), BF16),
            pltpu.VMEM((2, n_sa, rows, cols), BF16),
            pltpu.VMEM((n_sa, 2 * rows, 2 * cols), BF16),
        ] + sems,
        compiler_params=pltpu.CompilerParams(collective_id=0, has_side_effects=True),
        name="kadanoff",
    )(window, damping, propagator, coupling.reshape(1, no))


def solution(mesh):
    return jax.shard_map(
        shards,
        mesh=mesh,
        in_specs=(P(None, None, "sa", None, "tp"), P("sa", None), P(), P()),
        out_specs=P(None, "sa", None, "tp"),
        check_vma=False,
    )
```

```python
import functools
import math

import jax
import jax.numpy as jnp
from jax import lax
from jax.experimental import pallas as pl
from jax.experimental.pallas import tpu as pltpu
from jax.sharding import PartitionSpec as P

MESH = pl.DeviceIdType.MESH
F32 = jnp.float32
BF16 = jnp.bfloat16


def exact(a, b):
    return jnp.dot(a, b, precision=lax.Precision.HIGHEST, preferred_element_type=F32)


def split(x):
    high = x.astype(BF16)
    return high, (x - high.astype(F32)).astype(BF16)


def mm(a, b):
    return jnp.dot(a, b, preferred_element_type=F32)


def mm3(a, b):
    return mm(a[0], b[0]) + (mm(a[0], b[1]) + mm(a[1], b[0]))


def spectral_of(x_re, x_im, g_re, g_im, factor):
    lsquare_re = x_re * x_re - x_im * x_im
    lsquare_im = 2.0 * x_re * x_im
    gsquare_re = g_re * g_re - g_im * g_im
    gsquare_im = 2.0 * g_re * g_im
    sless_re = -factor * (lsquare_re * g_re + lsquare_im * g_im)
    sless_im = -factor * (lsquare_im * g_re - lsquare_re * g_im)
    sgreat_re = -factor * (gsquare_re * x_re + gsquare_im * x_im)
    sgreat_im = -factor * (gsquare_im * x_re - gsquare_re * x_im)
    return jnp.concatenate([sgreat_re - sless_re, sgreat_im - sless_im], axis=0).astype(BF16)


def low_lanes(x):
    return lax.broadcasted_iota(jnp.int32, x.shape, 1) < x.shape[1] // 2


def swap(x):
    return pltpu.roll(x, x.shape[1] // 2, 1)


def signed(x):
    return jnp.where(low_lanes(x), -x, x)


def pack(re, im):
    low = low_lanes(re)
    return jnp.where(low, re, swap(im)), jnp.where(low, swap(re), im)


def joined(a, b):
    return a + signed(swap(b))


def split_parts(x, no):
    n = x.shape[0] // (2 * no)
    y = x.reshape(n, 2, no, x.shape[1])
    return y[:, 0].reshape(n * no, x.shape[1]), y[:, 1].reshape(n * no, x.shape[1])


def spectral_packed(x, g, factor):
    low = low_lanes(x)
    xs, gs = swap(x), swap(g)
    x_re, x_im = jnp.where(low, x, xs), jnp.where(low, xs, x)
    g_re, g_im = jnp.where(low, g, gs), jnp.where(low, gs, g)
    z = x * g_re - signed(xs * g_im)
    return factor * (z * (x_re + signed(g_re)) + swap(z) * (signed(x_im) - g_im))


def kernel(
    n_sa, n_tp, scale,
    win_in, damp_in, prop_in, coup_in, out,
    win, damp, prop, coup, s_in, dall, hist, spec1, gst, gall, fst, fall, pmat, s2, pst, ps, y2, yst,
    s_d, r_d, s_h, r_h, s_k, r_k, s_g, r_g, s_s, r_s, s_f, r_f, s_p, r_p, s_q, r_q, s_y, r_y,
):
    me_sa = lax.axis_index("sa")
    me_tp = lax.axis_index("tp")
    no = prop.shape[1]
    cols = win.shape[4]
    rows = win.shape[2] * no
    core = lax.rem(me_sa, 2)
    pair = lax.div(me_sa, 2)
    sib = pair * 2 + 1 - core

    barrier = pltpu.get_barrier_semaphore()
    for k in range(1, n_tp):
        who = lax.rem(me_tp + k, n_tp)
        pl.semaphore_signal(barrier, inc=1, device_id=(me_sa, who), device_id_type=MESH)
        pl.semaphore_signal(barrier, inc=1, device_id=(sib, who), device_id_type=MESH)
    for k in range(1, n_sa):
        pl.semaphore_signal(
            barrier, inc=1, device_id=(lax.rem(me_sa + k, n_sa), me_tp), device_id_type=MESH
        )

    loads = [
        pltpu.make_async_copy(src, dst, s_in.at[n])
        for n, (src, dst) in enumerate(
            [(win_in, win), (coup_in, coup), (damp_in, damp), (prop_in, prop)]
        )
    ]
    for load in loads:
        load.start()

    pending = []

    def remote(src, dst, send, recv, dev):
        return pltpu.make_async_remote_copy(
            src_ref=src, dst_ref=dst, send_sem=send, recv_sem=recv,
            device_id=dev, device_id_type=MESH,
        )

    def push(src, dst, send, recv, dev):
        copy = remote(src, dst, send, recv, dev)
        copy.start()
        pending.append(copy)

    def send_sa(buf, send, recv):
        for k in range(1, n_sa):
            who = lax.rem(me_sa + k, n_sa)
            push(buf.at[me_sa], buf.at[me_sa], send.at[k - 1], recv.at[me_sa], (who, me_tp))

    def send_half(src, buf, send, recv):
        for k in range(1, n_sa):
            who = lax.rem(me_sa + k, n_sa)
            push(src.at[lax.rem(who, 2)], buf.at[me_sa], send.at[k - 1], recv.at[me_sa], (who, me_tp))

    def hand_on(source, n):
        half = hist.at[core, source]
        push(half, half, s_k.at[n], r_k.at[source], (sib, me_tp))

    def abroad():
        for k in range(1, n_sa // 2):
            other = lax.rem(pair + k, n_sa // 2) * 2
            yield other + core
            yield other + 1 - core

    def wait_sa(buf, send, recv):
        for k in range(1, n_sa):
            who = lax.rem(me_sa + k, n_sa)
            remote(buf.at[who], buf.at[who], send.at[k - 1], recv.at[who], (who, me_tp)).wait_recv()

    for load in loads:
        load.wait()

    row_id = lax.broadcasted_iota(jnp.int32, (no, cols), 0)
    lane_id = lax.broadcasted_iota(jnp.int32, (no, cols), 1)
    tiled = (lax.rem(lane_id, no) == row_id).astype(F32)
    c_row = coup[...]
    c_lanes = exact(c_row, tiled)
    eye = lax.broadcasted_iota(jnp.int32, (no, no), 0) == lax.broadcasted_iota(jnp.int32, (no, no), 1)
    c_col = jnp.sum(jnp.where(eye, jnp.broadcast_to(c_row, (no, no)), 0.0), axis=1, keepdims=True)
    factor = c_col * c_lanes
    factor2 = jnp.concatenate([factor] * win.shape[2], axis=0)

    l_re = win[0, 0].reshape(rows, cols)
    l_im = win[0, 1].reshape(rows, cols)
    g_re = win[1, 0].reshape(rows, cols)
    g_im = win[1, 1].reshape(rows, cols)
    spec1[me_tp] = spectral_of(l_re, l_im, g_re, g_im, factor2)
    l0, l1 = pack(l_re, l_im)
    hist[0, me_sa] = l0.astype(BF16)
    hist[1, me_sa] = l1.astype(BF16)
    dmine = dall.at[me_sa]
    dmine[...] = jnp.zeros(dmine.shape, F32)
    dmine[0:2, 0:no] = damp[...]
    g0, g1 = pack(g_re, g_im)
    gst[0] = g0.astype(BF16)
    gst[1] = g1.astype(BF16)
    gall[me_sa] = gst[core]

    pl.semaphore_wait(barrier, n_sa - 1 + 2 * (n_tp - 1))
    for k in range(1, n_tp):
        who = lax.rem(me_tp + k, n_tp)
        push(spec1.at[me_tp], spec1.at[me_tp], s_s.at[k - 1], r_s.at[me_tp], (me_sa, who))
    for k in range(1, n_sa):
        who = lax.rem(me_sa + k, n_sa)
        half = hist.at[lax.rem(who, 2), me_sa]
        push(half, half, s_h.at[k - 1], r_h.at[me_sa], (who, me_tp))
    hand_on(me_sa, 0)
    send_sa(dall, s_d, r_d)
    send_half(gst, gall, s_g, r_g)

    first = (lax.broadcasted_iota(jnp.int32, (no, 2 * no), 0)
             == lax.broadcasted_iota(jnp.int32, (no, 2 * no), 1)).astype(F32)
    second = (lax.broadcasted_iota(jnp.int32, (no, 2 * no), 0) + no
              == lax.broadcasted_iota(jnp.int32, (no, 2 * no), 1)).astype(F32)
    twice = (lax.rem(lax.broadcasted_iota(jnp.int32, (no, 4 * no), 1), 2 * no)
             == lax.broadcasted_iota(jnp.int32, (no, 4 * no), 0)).astype(F32)
    u_re, u_im = prop[0], prop[1]
    u_real = jnp.concatenate(
        [exact(u_re, first) - exact(u_im, second), exact(u_im, first) + exact(u_re, second)], axis=0
    )
    u_twice = jnp.concatenate([exact(u_re, twice), exact(u_im, twice)], axis=0)
    pick = (
        lax.rem(lax.broadcasted_iota(jnp.int32, (2 * no, 128), 0), no)
        == lax.broadcasted_iota(jnp.int32, (2 * no, 128), 1)
    )

    def damping_col(d_row):
        wide = jnp.broadcast_to(d_row, (2 * no, 128))
        return jnp.sum(jnp.where(pick, wide, 0.0), axis=1, keepdims=True)

    def begin(ref, l_packed):
        a0 = damping_col(ref[0:1, :]) * u_real
        prod = mm3(split(a0[:, 0:no]), split(l_packed))
        return joined_halves(prod[0:no], prod[no:])

    def joined_halves(a, b):
        return jnp.concatenate(
            [joined(a[:, 0:cols], b[:, 0:cols]), joined(a[:, cols:], b[:, cols:])], axis=1
        )

    start = begin(dmine, jnp.concatenate([l0[0:no], l1[0:no]], axis=1))
    start = jnp.where(me_sa == 0, start, jnp.zeros_like(start))
    start = jnp.concatenate([start, jnp.zeros((rows - no, 2 * cols), F32)], axis=0)

    for n, who in enumerate(abroad()):
        half = hist.at[core, who]
        remote(half, half, s_h.at[0], r_h.at[who], (who, me_tp)).wait_recv()
        hand_on(who, n + 1)
    half = hist.at[core, sib]
    remote(half, half, s_h.at[0], r_h.at[sib], (sib, me_tp)).wait_recv()
    half = hist.at[1 - core, sib]
    remote(half, half, s_k.at[0], r_k.at[sib], (sib, me_tp)).wait_recv()
    for who in abroad():
        half = hist.at[1 - core, who]
        remote(half, half, s_k.at[0], r_k.at[who], (sib, me_tp)).wait_recv()
    for k in range(1, n_tp):
        who = lax.rem(me_tp + k, n_tp)
        remote(spec1.at[who], spec1.at[who], s_s.at[k - 1], r_s.at[who], (me_sa, who)).wait_recv()
    history = jnp.concatenate([hist[h].reshape(n_sa * rows, cols) for h in range(2)], axis=1)
    acc = None
    for c in range(n_tp):
        part = mm(spec1[c], history[c * cols : (c + 1) * cols, :])
        acc = part if acc is None else acc + part
    force = scale * joined_halves(acc[0:rows], acc[rows:]) + start
    fst[0] = force[:, 0:cols].astype(BF16)
    fst[1] = force[:, cols:].astype(BF16)
    send_half(fst, fall, s_f, r_f)
    fall[me_sa] = fst[core]

    wait_sa(dall, s_d, r_d)
    ops = []
    for q in range(n_sa):
        d_odd = damping_col(dall[q, 1:2, :])
        even = damping_col(dall[q, 0:1, :]) * u_real
        both = exact(d_odd * u_real, even)
        ops.append((split(jnp.concatenate([even, both], axis=0)), d_odd * u_twice))

    lane = lax.broadcasted_iota(jnp.int32, (4 * no, 4 * no), 1)
    line = lax.broadcasted_iota(jnp.int32, (4 * no, 4 * no), 0)
    here = jnp.where(line < 2 * no, line, line - no)
    unit_rows = jnp.logical_or(line < no, jnp.logical_and(line >= 2 * no, line < 3 * no))
    def grow(q, last):
        (a_hi, a_lo), odd_cols = ops[q]
        at = (q % 2) * 2 * no
        placed = jnp.where(jnp.logical_and(unit_rows, lane == here + at), 1.0, 0.0)
        span = lax.broadcasted_iota(jnp.int32, (2 * no, 4 * no), 1)
        kept = jnp.where(jnp.logical_and(span >= at, span < at + no), odd_cols, 0.0)
        placed = placed + jnp.concatenate([jnp.zeros_like(kept), kept], axis=0)
        if q == 0:
            block = placed
        else:
            high, low = last
            wide = mm(jnp.concatenate([a_hi, a_lo], axis=0), high)
            moved = wide[0 : 4 * no] + (wide[4 * no :] + mm(a_hi, low))
            if q % 2 == 0:
                block = jnp.concatenate([moved, placed], axis=1)
            else:
                width = moved.shape[1] - 4 * no
                tail = moved[:, width:] + placed
                block = tail if width == 0 else jnp.concatenate([moved[:, 0:width], tail], axis=1)
        width = block.shape[1]
        pmat[q, :, 0:width] = block.astype(BF16)
        if width < n_sa * rows:
            pmat[q, :, width:] = jnp.zeros((4 * no, n_sa * rows - width), BF16)
        return split(block[2 * no :])

    def send_moved(start):
        at = 2 * me_tp + core
        for k in range(1, n_tp):
            who = lax.rem(me_tp + k, n_tp)
            start(remote(pst.at[core], ps.at[at], s_p.at[k - 1], r_p.at[at], (me_sa, who)))
            start(remote(pst.at[1 - core], ps.at[at], s_q.at[k - 1], r_p.at[at], (sib, who)))
        start(remote(pst.at[1 - core], ps.at[at], s_q.at[n_tp - 1], r_p.at[at], (sib, me_tp)))

    def apply(left, right):
        moved = joined(*split_parts(mm(left, right), no)).astype(BF16)
        pst[0] = moved[0:rows]
        pst[1] = moved[rows:]
        send_moved(lambda copy: copy.start())
        ps[2 * me_tp + core] = pst[core]

    def wait_forces(who):
        for buf, send, recv in ((gall, s_g, r_g), (fall, s_f, r_f)):
            remote(buf.at[who], buf.at[who], send.at[0], recv.at[who], (who, me_tp)).wait_recv()

    def wait_pair(j):
        wait_forces(2 * j)
        wait_forces(2 * j + 1)

    def predict(begin, end, spectral):
        depth = end * rows
        left = pmat[begin:end, :, 0:depth].reshape((end - begin) * 2 * rows, depth)
        x = joined(*split_parts(mm(left, fall[0:end].reshape(depth, cols)), no))
        y2[core, begin:end] = x.astype(BF16).reshape(end - begin, rows, cols)
        if spectral:
            g = gall[begin:end].reshape((end - begin) * rows, cols).astype(F32)
            wide = jnp.concatenate([factor2] * (end - begin), axis=0)
            s2[begin * rows : depth, :] = spectral_packed(x, g, wide).astype(BF16)

    groups = min(4, n_sa // 2)
    pairs = n_sa // 2 // groups
    unit = 2 * pairs
    group = lax.div(pair, pairs)
    last = None
    for n in range(groups):
        for q in range(n * unit, (n + 1) * unit):
            last = grow(q, last)

        @pl.when(group == n)
        def _():
            wait_forces(sib)
            for j in range((n + 1) * pairs):
                pl.when(pair != j)(functools.partial(wait_pair, j))
            for m in range(0, n + 1, 2):
                predict(m * unit, min(m + 2, n + 1) * unit, True)
            depth = (n + 1) * unit * rows
            apply(pmat[pl.ds(2 * pair, 2), :, 0:depth].reshape(4 * rows, depth), s2[0:depth])

    for n in range(groups - 1):

        @pl.when(group == n)
        def _():
            for j in range((n + 1) * pairs, n_sa // 2):
                wait_pair(j)
            for m in range(n + 1, groups, 2):
                predict(m * unit, min(m + 2, groups) * unit, False)

    push(y2.at[core], y2.at[core], s_y.at[0], r_y.at[0], (sib, me_tp))
    first_rows = jnp.concatenate([hist[h, 0, 0:no] for h in range(2)], axis=1).astype(F32)
    q_left = pmat[me_sa][:, 0:no]
    q_own = mm(q_left, begin(dall.at[0], first_rows).astype(BF16))
    q_own = joined_halves(*split_parts(q_own, no))

    remote(y2.at[1 - core], y2.at[1 - core], s_y.at[0], r_y.at[0], (sib, me_tp)).wait_recv()
    for h in range(2):
        y = y2[h]
        turned = signed(swap(y.reshape(n_sa * rows, cols).astype(F32))).astype(BF16)
        yst[:, 0:rows, h * cols : (h + 1) * cols] = y
        yst[:, rows:, h * cols : (h + 1) * cols] = turned.reshape(n_sa, rows, cols)
    base = 0.5 * (jnp.concatenate([y2[0, me_sa], y2[1, me_sa]], axis=1).astype(F32) + q_own)

    for k in range(n_tp):
        who = lax.rem(me_tp + k, n_tp)
        for h in (core, 1 - core):
            if k == 0 and h is core:
                continue
            at = 2 * who + h
            remote(ps.at[at], ps.at[at], s_p.at[0], r_p.at[at], (me_sa, who)).wait_recv()
    left = jnp.concatenate([ps[n] for n in range(2 * n_tp)], axis=1)
    final = base + (0.5 * scale) * mm(left, yst[...].reshape(2 * n_sa * rows, 2 * cols))
    f0, f1 = final[:, 0:cols], final[:, cols:]
    low = low_lanes(f0)
    out[0] = jnp.where(low, f0, swap(f1)).reshape(win.shape[2], no, cols)
    out[1] = jnp.where(low, swap(f0), f1).reshape(win.shape[2], no, cols)
    for copy in pending:
        copy.wait_send()
    send_moved(lambda copy: copy.wait_send())


def shards(window, damping, propagator, coupling):
    n_sa, n_tp = lax.axis_size("sa"), lax.axis_size("tp")
    no = coupling.shape[0]
    block = window.shape[2]
    cols = window.shape[4]
    rows = block * no
    scale = 1.0 / (block * n_sa * math.sqrt(no))
    dma = lambda n: pltpu.SemaphoreType.DMA((n,))
    vm = pl.BlockSpec(memory_space=pltpu.VMEM)
    sems = []
    for n, m in ((n_sa, n_sa), (n_sa, n_sa), (n_sa, n_sa), (n_sa, n_sa), (n_tp, n_tp), (n_sa, n_sa),
                 (n_tp, 2 * n_tp), (n_tp, 1), (1, 1)):
        sems += [dma(n), dma(m)]
    return pl.pallas_call(
        functools.partial(kernel, n_sa, n_tp, scale),
        out_shape=pltpu.VMEM((2, block, no, cols), F32),
        in_specs=[pl.BlockSpec(memory_space=pl.ANY)] * 4,
        out_specs=vm,
        scratch_shapes=[
            pltpu.VMEM(window.shape, F32),
            pltpu.VMEM(damping.shape, F32),
            pltpu.VMEM(propagator.shape, F32),
            pltpu.VMEM((1, no), F32),
            dma(4),
            pltpu.VMEM((n_sa, 8, 128), F32),
            pltpu.VMEM((2, n_sa, rows, cols), BF16),
            pltpu.VMEM((n_tp, 2 * rows, cols), BF16),
            pltpu.VMEM((2, rows, cols), BF16),
            pltpu.VMEM((n_sa, rows, cols), BF16),
            pltpu.VMEM((2, rows, cols), BF16),
            pltpu.VMEM((n_sa, rows, cols), BF16),
            pltpu.VMEM((n_sa, 2 * rows, n_sa * rows), BF16),
            pltpu.VMEM((n_sa * rows, cols), BF16),
            pltpu.VMEM((2, rows, cols), BF16),
            pltpu.VMEM((2 * n_tp, rows, cols), BF16),
            pltpu.VMEM((2, n_sa, rows, cols), BF16),
            pltpu.VMEM((n_sa, 2 * rows, 2 * cols), BF16),
        ] + sems,
        compiler_params=pltpu.CompilerParams(collective_id=0, has_side_effects=True),
        name="kadanoff",
    )(window, damping, propagator, coupling.reshape(1, no))


def solution(mesh):
    return jax.shard_map(
        shards,
        mesh=mesh,
        in_specs=(P(None, None, "sa", None, "tp"), P("sa", None), P(), P()),
        out_specs=P(None, "sa", None, "tp"),
        check_vma=False,
    )
```

```python
import functools
import math

import jax
import jax.numpy as jnp
from jax import lax
from jax.experimental import pallas as pl
from jax.experimental.pallas import tpu as pltpu
from jax.sharding import PartitionSpec as P

MESH = pl.DeviceIdType.MESH
F32 = jnp.float32
BF16 = jnp.bfloat16


def exact(a, b):
    return jnp.dot(a, b, precision=lax.Precision.HIGHEST, preferred_element_type=F32)


def split(x):
    high = x.astype(BF16)
    return high, (x - high.astype(F32)).astype(BF16)


def mm(a, b):
    return jnp.dot(a, b, preferred_element_type=F32)


def mm3(a, b):
    return mm(a[0], b[0]) + (mm(a[0], b[1]) + mm(a[1], b[0]))


def spectral_of(x_re, x_im, g_re, g_im, factor):
    lsquare_re = x_re * x_re - x_im * x_im
    lsquare_im = 2.0 * x_re * x_im
    gsquare_re = g_re * g_re - g_im * g_im
    gsquare_im = 2.0 * g_re * g_im
    sless_re = -factor * (lsquare_re * g_re + lsquare_im * g_im)
    sless_im = -factor * (lsquare_im * g_re - lsquare_re * g_im)
    sgreat_re = -factor * (gsquare_re * x_re + gsquare_im * x_im)
    sgreat_im = -factor * (gsquare_im * x_re - gsquare_re * x_im)
    return jnp.concatenate([sgreat_re - sless_re, sgreat_im - sless_im], axis=0).astype(BF16)


def low_lanes(x):
    return lax.broadcasted_iota(jnp.int32, x.shape, 1) < x.shape[1] // 2


def swap(x):
    return pltpu.roll(x, x.shape[1] // 2, 1)


def signed(x):
    return jnp.where(low_lanes(x), -x, x)


def pack(re, im):
    low = low_lanes(re)
    return jnp.where(low, re, swap(im)), jnp.where(low, swap(re), im)


def joined(a, b):
    return a + signed(swap(b))


def split_parts(x, no):
    n = x.shape[0] // (2 * no)
    y = x.reshape(n, 2, no, x.shape[1])
    return y[:, 0].reshape(n * no, x.shape[1]), y[:, 1].reshape(n * no, x.shape[1])


def spectral_packed(x, g, factor):
    low = low_lanes(x)
    xs, gs = swap(x), swap(g)
    x_re, x_im = jnp.where(low, x, xs), jnp.where(low, xs, x)
    g_re, g_im = jnp.where(low, g, gs), jnp.where(low, gs, g)
    z = x * g_re - signed(xs * g_im)
    return factor * (z * (x_re + signed(g_re)) + swap(z) * (signed(x_im) - g_im))


def kernel(
    n_sa, n_tp, scale,
    win_in, damp_in, prop_in, coup_in, out,
    win, damp, prop, coup, s_in, dall, hist, spec1, gst, gall, fst, fall, pmat, s2, pst, ps, y2, yst,
    s_d, r_d, s_h, r_h, s_k, r_k, s_g, r_g, s_s, r_s, s_f, r_f, s_p, r_p, s_y, r_y,
):
    me_sa = lax.axis_index("sa")
    me_tp = lax.axis_index("tp")
    no = prop.shape[1]
    cols = win.shape[4]
    rows = win.shape[2] * no
    core = lax.rem(me_sa, 2)
    pair = lax.div(me_sa, 2)
    sib = pair * 2 + 1 - core

    barrier = pltpu.get_barrier_semaphore()
    for k in range(1, n_tp):
        who = lax.rem(me_tp + k, n_tp)
        pl.semaphore_signal(barrier, inc=1, device_id=(me_sa, who), device_id_type=MESH)
        pl.semaphore_signal(barrier, inc=1, device_id=(sib, who), device_id_type=MESH)
    for k in range(1, n_sa):
        pl.semaphore_signal(
            barrier, inc=1, device_id=(lax.rem(me_sa + k, n_sa), me_tp), device_id_type=MESH
        )

    loads = [
        pltpu.make_async_copy(src, dst, s_in.at[n])
        for n, (src, dst) in enumerate(
            [(win_in, win), (coup_in, coup), (damp_in, damp), (prop_in, prop)]
        )
    ]
    for load in loads:
        load.start()

    def remote(src, dst, send, recv, dev):
        return pltpu.make_async_remote_copy(
            src_ref=src, dst_ref=dst, send_sem=send, recv_sem=recv,
            device_id=dev, device_id_type=MESH,
        )

    def arrived(block, recv):
        remote(block, block, s_y, recv, (sib, me_tp)).wait_recv()

    def left_here(block, send):
        remote(block, block, send, r_y, (sib, me_tp)).wait_send()

    def send_half(src, dst, send, recv):
        for k in range(1, n_sa):
            who = lax.rem(me_sa + k, n_sa)
            remote(src(lax.rem(who, 2)), dst(lax.rem(who, 2)), send, recv, (who, me_tp)).start()

    def hand_on(block):
        remote(block, block, s_k, r_k, (sib, me_tp)).start()

    for load in loads:
        load.wait()

    row_id = lax.broadcasted_iota(jnp.int32, (no, cols), 0)
    lane_id = lax.broadcasted_iota(jnp.int32, (no, cols), 1)
    tiled = (lax.rem(lane_id, no) == row_id).astype(F32)
    c_row = coup[...]
    c_lanes = exact(c_row, tiled)
    eye = lax.broadcasted_iota(jnp.int32, (no, no), 0) == lax.broadcasted_iota(jnp.int32, (no, no), 1)
    c_col = jnp.sum(jnp.where(eye, jnp.broadcast_to(c_row, (no, no)), 0.0), axis=1, keepdims=True)
    factor = c_col * c_lanes
    factor2 = jnp.concatenate([factor] * win.shape[2], axis=0)

    l_re = win[0, 0].reshape(rows, cols)
    l_im = win[0, 1].reshape(rows, cols)
    g_re = win[1, 0].reshape(rows, cols)
    g_im = win[1, 1].reshape(rows, cols)
    spec1[me_tp] = spectral_of(l_re, l_im, g_re, g_im, factor2)
    l0, l1 = pack(l_re, l_im)
    hist[0, me_sa] = l0.astype(BF16)
    hist[1, me_sa] = l1.astype(BF16)
    dmine = dall.at[me_sa]
    dmine[...] = jnp.zeros(dmine.shape, F32)
    dmine[0:2, 0:no] = damp[...]
    g0, g1 = pack(g_re, g_im)
    gst[0] = g0.astype(BF16)
    gst[1] = g1.astype(BF16)
    gall[me_sa] = gst[core]

    pl.semaphore_wait(barrier, n_sa - 1 + 2 * (n_tp - 1))
    for k in range(1, n_tp):
        who = lax.rem(me_tp + k, n_tp)
        remote(spec1.at[me_tp], spec1.at[me_tp], s_s, r_s, (me_sa, who)).start()
    own_half = lambda half: hist.at[half, me_sa]
    send_half(own_half, own_half, s_h, r_h.at[pair])
    hand_on(hist.at[core, me_sa])
    for k in range(1, n_sa):
        who = lax.rem(me_sa + k, n_sa)
        remote(dall.at[me_sa], dall.at[me_sa], s_d, r_d, (who, me_tp)).start()
    send_half(lambda half: gst.at[half], lambda half: gall.at[me_sa], s_g, r_g)

    first = (lax.broadcasted_iota(jnp.int32, (no, 2 * no), 0)
             == lax.broadcasted_iota(jnp.int32, (no, 2 * no), 1)).astype(F32)
    second = (lax.broadcasted_iota(jnp.int32, (no, 2 * no), 0) + no
              == lax.broadcasted_iota(jnp.int32, (no, 2 * no), 1)).astype(F32)
    twice = (lax.rem(lax.broadcasted_iota(jnp.int32, (no, 4 * no), 1), 2 * no)
             == lax.broadcasted_iota(jnp.int32, (no, 4 * no), 0)).astype(F32)
    u_re, u_im = prop[0], prop[1]
    u_real = jnp.concatenate(
        [exact(u_re, first) - exact(u_im, second), exact(u_im, first) + exact(u_re, second)], axis=0
    )
    u_twice = jnp.concatenate([exact(u_re, twice), exact(u_im, twice)], axis=0)
    pick = (
        lax.rem(lax.broadcasted_iota(jnp.int32, (2 * no, 128), 0), no)
        == lax.broadcasted_iota(jnp.int32, (2 * no, 128), 1)
    )

    def damping_col(d_row):
        wide = jnp.broadcast_to(d_row, (2 * no, 128))
        return jnp.sum(jnp.where(pick, wide, 0.0), axis=1, keepdims=True)

    def begin(ref, l_packed):
        a0 = damping_col(ref[0:1, :]) * u_real
        prod = mm3(split(a0[:, 0:no]), split(l_packed))
        return joined_halves(prod[0:no], prod[no:])

    def joined_halves(a, b):
        return jnp.concatenate(
            [joined(a[:, 0:cols], b[:, 0:cols]), joined(a[:, cols:], b[:, cols:])], axis=1
        )

    start = begin(dmine, jnp.concatenate([l0[0:no], l1[0:no]], axis=1))
    start = jnp.where(me_sa == 0, start, jnp.zeros_like(start))
    start = jnp.concatenate([start, jnp.zeros((rows - no, 2 * cols), F32)], axis=0)

    for k in range(1, n_sa // 2):
        other = lax.rem(pair + k, n_sa // 2)
        both = hist.at[core, pl.ds(2 * other, 2)]
        arrived(both, r_h.at[other])
        hand_on(both)
    arrived(hist.at[core, sib], r_h.at[pair])
    arrived(hist.at[1 - core, 0 : n_sa - 1], r_k)
    arrived(spec1.at[0 : n_tp - 1], r_s)
    history = jnp.concatenate([hist[h].reshape(n_sa * rows, cols) for h in range(2)], axis=1)
    acc = None
    for c in range(n_tp):
        part = mm(spec1[c], history[c * cols : (c + 1) * cols, :])
        acc = part if acc is None else acc + part
    force = scale * joined_halves(acc[0:rows], acc[rows:]) + start
    fst[0] = force[:, 0:cols].astype(BF16)
    fst[1] = force[:, cols:].astype(BF16)
    send_half(lambda half: fst.at[half], lambda half: fall.at[me_sa], s_f, r_f.at[pair])
    fall[me_sa] = fst[core]

    arrived(dall.at[0 : n_sa - 1], r_d)
    ops = []
    for q in range(n_sa):
        d_odd = damping_col(dall[q, 1:2, :])
        even = damping_col(dall[q, 0:1, :]) * u_real
        both = exact(d_odd * u_real, even)
        ops.append((split(jnp.concatenate([even, both], axis=0)), d_odd * u_twice))

    lane = lax.broadcasted_iota(jnp.int32, (4 * no, 4 * no), 1)
    line = lax.broadcasted_iota(jnp.int32, (4 * no, 4 * no), 0)
    here = jnp.where(line < 2 * no, line, line - no)
    unit_rows = jnp.logical_or(line < no, jnp.logical_and(line >= 2 * no, line < 3 * no))
    def grow(q, last):
        (a_hi, a_lo), odd_cols = ops[q]
        at = (q % 2) * 2 * no
        placed = jnp.where(jnp.logical_and(unit_rows, lane == here + at), 1.0, 0.0)
        span = lax.broadcasted_iota(jnp.int32, (2 * no, 4 * no), 1)
        kept = jnp.where(jnp.logical_and(span >= at, span < at + no), odd_cols, 0.0)
        placed = placed + jnp.concatenate([jnp.zeros_like(kept), kept], axis=0)
        if q == 0:
            block = placed
        else:
            high, low = last
            wide = mm(jnp.concatenate([a_hi, a_lo], axis=0), high)
            moved = wide[0 : 4 * no] + (wide[4 * no :] + mm(a_hi, low))
            if q % 2 == 0:
                block = jnp.concatenate([moved, placed], axis=1)
            else:
                width = moved.shape[1] - 4 * no
                tail = moved[:, width:] + placed
                block = tail if width == 0 else jnp.concatenate([moved[:, 0:width], tail], axis=1)
        width = block.shape[1]
        pmat[q, :, 0:width] = block.astype(BF16)
        if width < n_sa * rows:
            pmat[q, :, width:] = jnp.zeros((4 * no, n_sa * rows - width), BF16)
        return split(block[2 * no :])

    def send_moved():
        mine = ps.at[2 * me_tp + core]
        for k in range(1, n_tp):
            who = lax.rem(me_tp + k, n_tp)
            remote(pst.at[core], mine, s_p, r_p, (me_sa, who)).start()
            remote(pst.at[1 - core], mine, s_p, r_p, (sib, who)).start()
        remote(pst.at[1 - core], mine, s_p, r_p, (sib, me_tp)).start()

    def apply(left, right):
        moved = joined(*split_parts(mm(left, right), no)).astype(BF16)
        pst[0] = moved[0:rows]
        pst[1] = moved[rows:]
        send_moved()
        ps[2 * me_tp + core] = pst[core]

    def wait_pair(j):
        arrived(fall.at[2 * j : 2 * j + 2], r_f.at[j])

    def predict(begin, end, spectral):
        depth = end * rows
        left = pmat[begin:end, :, 0:depth].reshape((end - begin) * 2 * rows, depth)
        x = joined(*split_parts(mm(left, fall[0:end].reshape(depth, cols)), no))
        y2[core, begin:end] = x.astype(BF16).reshape(end - begin, rows, cols)
        if spectral:
            g = gall[begin:end].reshape((end - begin) * rows, cols).astype(F32)
            wide = jnp.concatenate([factor2] * (end - begin), axis=0)
            s2[begin * rows : depth, :] = spectral_packed(x, g, wide).astype(BF16)

    groups = min(4, n_sa // 2)
    pairs = n_sa // 2 // groups
    unit = 2 * pairs
    group = lax.div(pair, pairs)
    last = None
    for n in range(groups):
        for q in range(n * unit, (n + 1) * unit):
            last = grow(q, last)

        @pl.when(group == n)
        def _():
            arrived(gall.at[0 : n_sa - 1], r_g)
            arrived(fall.at[sib], r_f.at[pair])
            for j in range((n + 1) * pairs):
                pl.when(pair != j)(functools.partial(wait_pair, j))
            for m in range(0, n + 1, 2):
                predict(m * unit, min(m + 2, n + 1) * unit, True)
            depth = (n + 1) * unit * rows
            apply(pmat[pl.ds(2 * pair, 2), :, 0:depth].reshape(4 * rows, depth), s2[0:depth])

    for n in range(groups - 1):

        @pl.when(group == n)
        def _():
            for j in range((n + 1) * pairs, n_sa // 2):
                wait_pair(j)
            for m in range(n + 1, groups, 2):
                predict(m * unit, min(m + 2, groups) * unit, False)

    remote(y2.at[core], y2.at[core], s_y, r_y, (sib, me_tp)).start()
    first_rows = jnp.concatenate([hist[h, 0, 0:no] for h in range(2)], axis=1).astype(F32)
    q_left = pmat[me_sa][:, 0:no]
    q_own = mm(q_left, begin(dall.at[0], first_rows).astype(BF16))
    q_own = joined_halves(*split_parts(q_own, no))

    arrived(y2.at[1 - core], r_y)
    for h in range(2):
        y = y2[h]
        turned = signed(swap(y.reshape(n_sa * rows, cols).astype(F32))).astype(BF16)
        yst[:, 0:rows, h * cols : (h + 1) * cols] = y
        yst[:, rows:, h * cols : (h + 1) * cols] = turned.reshape(n_sa, rows, cols)
    base = 0.5 * (jnp.concatenate([y2[0, me_sa], y2[1, me_sa]], axis=1).astype(F32) + q_own)

    arrived(ps.at[0 : 2 * n_tp - 1], r_p)
    left = jnp.concatenate([ps[n] for n in range(2 * n_tp)], axis=1)
    final = base + (0.5 * scale) * mm(left, yst[...].reshape(2 * n_sa * rows, 2 * cols))
    f0, f1 = final[:, 0:cols], final[:, cols:]
    low = low_lanes(f0)
    out[0] = jnp.where(low, f0, swap(f1)).reshape(win.shape[2], no, cols)
    out[1] = jnp.where(low, swap(f0), f1).reshape(win.shape[2], no, cols)
    left_here(spec1.at[0 : n_tp - 1], s_s)
    left_here(dall.at[0 : n_sa - 1], s_d)
    for send in (s_h, s_k, s_g, s_f):
        left_here(gall.at[0 : n_sa - 1], send)
    left_here(ps.at[0 : 2 * n_tp - 1], s_p)
    left_here(y2.at[core], s_y)


def shards(window, damping, propagator, coupling):
    n_sa, n_tp = lax.axis_size("sa"), lax.axis_size("tp")
    no = coupling.shape[0]
    block = window.shape[2]
    cols = window.shape[4]
    rows = block * no
    scale = 1.0 / (block * n_sa * math.sqrt(no))
    dma = lambda n: pltpu.SemaphoreType.DMA((n,))
    vm = pl.BlockSpec(memory_space=pltpu.VMEM)
    one = pltpu.SemaphoreType.DMA
    sems = [
        one, one, one, dma(n_sa // 2), one, one, one, one,
        one, one, one, dma(n_sa // 2), one, one, one, one,
    ]
    return pl.pallas_call(
        functools.partial(kernel, n_sa, n_tp, scale),
        out_shape=pltpu.VMEM((2, block, no, cols), F32),
        in_specs=[pl.BlockSpec(memory_space=pl.ANY)] * 4,
        out_specs=vm,
        scratch_shapes=[
            pltpu.VMEM(window.shape, F32),
            pltpu.VMEM(damping.shape, F32),
            pltpu.VMEM(propagator.shape, F32),
            pltpu.VMEM((1, no), F32),
            dma(4),
            pltpu.VMEM((n_sa, 8, 128), F32),
            pltpu.VMEM((2, n_sa, rows, cols), BF16),
            pltpu.VMEM((n_tp, 2 * rows, cols), BF16),
            pltpu.VMEM((2, rows, cols), BF16),
            pltpu.VMEM((n_sa, rows, cols), BF16),
            pltpu.VMEM((2, rows, cols), BF16),
            pltpu.VMEM((n_sa, rows, cols), BF16),
            pltpu.VMEM((n_sa, 2 * rows, n_sa * rows), BF16),
            pltpu.VMEM((n_sa * rows, cols), BF16),
            pltpu.VMEM((2, rows, cols), BF16),
            pltpu.VMEM((2 * n_tp, rows, cols), BF16),
            pltpu.VMEM((2, n_sa, rows, cols), BF16),
            pltpu.VMEM((n_sa, 2 * rows, 2 * cols), BF16),
        ] + sems,
        compiler_params=pltpu.CompilerParams(collective_id=0, has_side_effects=True),
        name="kadanoff",
    )(window, damping, propagator, coupling.reshape(1, no))


def solution(mesh):
    return jax.shard_map(
        shards,
        mesh=mesh,
        in_specs=(P(None, None, "sa", None, "tp"), P("sa", None), P(), P()),
        out_specs=P(None, "sa", None, "tp"),
        check_vma=False,
    )
```

```python
import functools
import math

import jax
import jax.numpy as jnp
from jax import lax
from jax.experimental import pallas as pl
from jax.experimental.pallas import tpu as pltpu
from jax.sharding import PartitionSpec as P

MESH = pl.DeviceIdType.MESH
F32 = jnp.float32
BF16 = jnp.bfloat16


def exact(a, b):
    return jnp.dot(a, b, precision=lax.Precision.HIGHEST, preferred_element_type=F32)


def split(x):
    high = x.astype(BF16)
    return high, (x - high.astype(F32)).astype(BF16)


def mm(a, b):
    return jnp.dot(a, b, preferred_element_type=F32)


def mm3(a, b):
    return mm(a[0], b[0]) + (mm(a[0], b[1]) + mm(a[1], b[0]))


def spectral_of(x_re, x_im, g_re, g_im, factor):
    lsquare_re = x_re * x_re - x_im * x_im
    lsquare_im = 2.0 * x_re * x_im
    gsquare_re = g_re * g_re - g_im * g_im
    gsquare_im = 2.0 * g_re * g_im
    sless_re = -factor * (lsquare_re * g_re + lsquare_im * g_im)
    sless_im = -factor * (lsquare_im * g_re - lsquare_re * g_im)
    sgreat_re = -factor * (gsquare_re * x_re + gsquare_im * x_im)
    sgreat_im = -factor * (gsquare_im * x_re - gsquare_re * x_im)
    return jnp.concatenate([sgreat_re - sless_re, sgreat_im - sless_im], axis=0).astype(BF16)


def low_lanes(x):
    return lax.broadcasted_iota(jnp.int32, x.shape, 1) < x.shape[1] // 2


def swap(x):
    return pltpu.roll(x, x.shape[1] // 2, 1)


def signed(x):
    return jnp.where(low_lanes(x), -x, x)


def pack(re, im):
    low = low_lanes(re)
    return jnp.where(low, re, swap(im)), jnp.where(low, swap(re), im)


def joined(a, b):
    return a + signed(swap(b))


def split_parts(x, no):
    n = x.shape[0] // (2 * no)
    y = x.reshape(n, 2, no, x.shape[1])
    return y[:, 0].reshape(n * no, x.shape[1]), y[:, 1].reshape(n * no, x.shape[1])


def spectral_packed(x, g, factor):
    low = low_lanes(x)
    xs, gs = swap(x), swap(g)
    x_re, x_im = jnp.where(low, x, xs), jnp.where(low, xs, x)
    g_re, g_im = jnp.where(low, g, gs), jnp.where(low, gs, g)
    z = x * g_re - signed(xs * g_im)
    return factor * (z * (x_re + signed(g_re)) + swap(z) * (signed(x_im) - g_im))


def kernel(
    n_sa, n_tp, scale,
    win_in, damp_in, prop_in, coup_in, out,
    win, damp, prop, coup, s_in, dall, hist, spec1, gst, gall, fst, fall, pmat, s2, pst, ps, y2, yst,
    s_d, r_d, s_h, r_h, s_k, r_k, s_g, r_g, s_s, r_s, s_f, r_f, s_p, r_p, s_y, r_y,
):
    me_sa = lax.axis_index("sa")
    me_tp = lax.axis_index("tp")
    no = prop.shape[1]
    cols = win.shape[4]
    rows = win.shape[2] * no
    core = lax.rem(me_sa, 2)
    pair = lax.div(me_sa, 2)
    sib = pair * 2 + 1 - core

    barrier = pltpu.get_barrier_semaphore()
    def far(k):
        down = n_tp - k - (me_tp >= n_tp - k).astype(jnp.int32)
        up = k - 1 + (me_tp <= k - 1).astype(jnp.int32)
        return jnp.where(2 * me_tp < n_tp, down, up)

    def greet(sa, tp):
        pl.semaphore_signal(barrier, inc=1, device_id=(sa, tp), device_id_type=MESH)

    for k in range(1, n_tp):
        greet(me_sa, far(k))
    for k in range(1, n_sa):
        greet(lax.rem(me_sa + k, n_sa), me_tp)
    for k in range(1, n_tp):
        greet(sib, far(k))

    loads = [
        pltpu.make_async_copy(src, dst, s_in.at[n])
        for n, (src, dst) in enumerate(
            [(win_in, win), (coup_in, coup), (damp_in, damp), (prop_in, prop)]
        )
    ]
    for load in loads:
        load.start()

    def remote(src, dst, send, recv, dev):
        return pltpu.make_async_remote_copy(
            src_ref=src, dst_ref=dst, send_sem=send, recv_sem=recv,
            device_id=dev, device_id_type=MESH,
        )

    def arrived(block, recv):
        remote(block, block, s_y, recv, (sib, me_tp)).wait_recv()

    def left_here(block, send):
        remote(block, block, send, r_y, (sib, me_tp)).wait_send()

    def send_half(src, dst, send, recv):
        for k in range(1, n_sa):
            who = lax.rem(me_sa + k, n_sa)
            remote(src(lax.rem(who, 2)), dst(lax.rem(who, 2)), send, recv, (who, me_tp)).start()

    def hand_on(block):
        remote(block, block, s_k, r_k, (sib, me_tp)).start()

    for load in loads:
        load.wait()

    row_id = lax.broadcasted_iota(jnp.int32, (no, cols), 0)
    lane_id = lax.broadcasted_iota(jnp.int32, (no, cols), 1)
    tiled = (lax.rem(lane_id, no) == row_id).astype(F32)
    c_row = coup[...]
    c_lanes = exact(c_row, tiled)
    eye = lax.broadcasted_iota(jnp.int32, (no, no), 0) == lax.broadcasted_iota(jnp.int32, (no, no), 1)
    c_col = jnp.sum(jnp.where(eye, jnp.broadcast_to(c_row, (no, no)), 0.0), axis=1, keepdims=True)
    factor = c_col * c_lanes
    factor2 = jnp.concatenate([factor] * win.shape[2], axis=0)

    l_re = win[0, 0].reshape(rows, cols)
    l_im = win[0, 1].reshape(rows, cols)
    g_re = win[1, 0].reshape(rows, cols)
    g_im = win[1, 1].reshape(rows, cols)
    spec1[me_tp] = spectral_of(l_re, l_im, g_re, g_im, factor2)
    l0, l1 = pack(l_re, l_im)
    hist[0, me_sa] = l0.astype(BF16)
    hist[1, me_sa] = l1.astype(BF16)
    dmine = dall.at[me_sa]
    dmine[...] = jnp.zeros(dmine.shape, F32)
    dmine[0:1, 0:no] = damp[0:1, :]
    dmine[0:1, no : 2 * no] = damp[1:2, :]
    g0, g1 = pack(g_re, g_im)
    gst[0] = g0.astype(BF16)
    gst[1] = g1.astype(BF16)
    gall[me_sa] = gst[core]

    pl.semaphore_wait(barrier, n_sa - 1 + 2 * (n_tp - 1))
    for k in range(1, n_tp):
        who = far(k)
        remote(spec1.at[me_tp], spec1.at[me_tp], s_s, r_s, (me_sa, who)).start()
    own_half = lambda half: hist.at[half, me_sa]
    send_half(own_half, own_half, s_h, r_h.at[pair])
    hand_on(hist.at[core, me_sa])
    for k in range(1, n_sa):
        who = lax.rem(me_sa + k, n_sa)
        remote(dall.at[me_sa, 0:1], dall.at[me_sa, 0:1], s_d, r_d, (who, me_tp)).start()
    send_half(lambda half: gst.at[half], lambda half: gall.at[me_sa], s_g, r_g)

    first = (lax.broadcasted_iota(jnp.int32, (no, 2 * no), 0)
             == lax.broadcasted_iota(jnp.int32, (no, 2 * no), 1)).astype(F32)
    second = (lax.broadcasted_iota(jnp.int32, (no, 2 * no), 0) + no
              == lax.broadcasted_iota(jnp.int32, (no, 2 * no), 1)).astype(F32)
    twice = (lax.rem(lax.broadcasted_iota(jnp.int32, (no, 4 * no), 1), 2 * no)
             == lax.broadcasted_iota(jnp.int32, (no, 4 * no), 0)).astype(F32)
    u_re, u_im = prop[0], prop[1]
    u_real = jnp.concatenate(
        [exact(u_re, first) - exact(u_im, second), exact(u_im, first) + exact(u_re, second)], axis=0
    )
    u_twice = jnp.concatenate([exact(u_re, twice), exact(u_im, twice)], axis=0)
    orbital = lax.rem(lax.broadcasted_iota(jnp.int32, (2 * no, 128), 0), no)
    column = lax.broadcasted_iota(jnp.int32, (2 * no, 128), 1)

    def damping_col(ref, n):
        wide = jnp.broadcast_to(ref[0:1, :], (2 * no, 128))
        return jnp.sum(jnp.where(column == orbital + n * no, wide, 0.0), axis=1, keepdims=True)

    def begin(ref, l_packed):
        a0 = damping_col(ref, 0) * u_real
        prod = mm3(split(a0[:, 0:no]), split(l_packed))
        return joined_halves(prod[0:no], prod[no:])

    def joined_halves(a, b):
        return jnp.concatenate(
            [joined(a[:, 0:cols], b[:, 0:cols]), joined(a[:, cols:], b[:, cols:])], axis=1
        )

    start = begin(dmine, jnp.concatenate([l0[0:no], l1[0:no]], axis=1))
    start = jnp.where(me_sa == 0, start, jnp.zeros_like(start))
    start = jnp.concatenate([start, jnp.zeros((rows - no, 2 * cols), F32)], axis=0)

    for k in range(1, n_sa // 2):
        other = lax.rem(pair + k, n_sa // 2)
        both = hist.at[core, pl.ds(2 * other, 2)]
        arrived(both, r_h.at[other])
        hand_on(both)
    arrived(hist.at[core, sib], r_h.at[pair])
    arrived(hist.at[1 - core, 0 : n_sa - 1], r_k)
    arrived(spec1.at[0 : n_tp - 1], r_s)
    history = jnp.concatenate([hist[h].reshape(n_sa * rows, cols) for h in range(2)], axis=1)
    acc = None
    for c in range(n_tp):
        part = mm(spec1[c], history[c * cols : (c + 1) * cols, :])
        acc = part if acc is None else acc + part
    force = scale * joined_halves(acc[0:rows], acc[rows:]) + start
    fst[0] = force[:, 0:cols].astype(BF16)
    fst[1] = force[:, cols:].astype(BF16)
    send_half(lambda half: fst.at[half], lambda half: fall.at[me_sa], s_f, r_f.at[pair])
    fall[me_sa] = fst[core]

    arrived(dall.at[0 : n_sa - 1, 0:1], r_d)
    ops = []
    for q in range(n_sa):
        d_odd = damping_col(dall.at[q], 1)
        even = damping_col(dall.at[q], 0) * u_real
        both = exact(d_odd * u_real, even)
        ops.append((split(jnp.concatenate([even, both], axis=0)), d_odd * u_twice))

    lane = lax.broadcasted_iota(jnp.int32, (4 * no, 4 * no), 1)
    line = lax.broadcasted_iota(jnp.int32, (4 * no, 4 * no), 0)
    here = jnp.where(line < 2 * no, line, line - no)
    unit_rows = jnp.logical_or(line < no, jnp.logical_and(line >= 2 * no, line < 3 * no))
    def grow(q, last):
        (a_hi, a_lo), odd_cols = ops[q]
        at = (q % 2) * 2 * no
        placed = jnp.where(jnp.logical_and(unit_rows, lane == here + at), 1.0, 0.0)
        span = lax.broadcasted_iota(jnp.int32, (2 * no, 4 * no), 1)
        kept = jnp.where(jnp.logical_and(span >= at, span < at + no), odd_cols, 0.0)
        placed = placed + jnp.concatenate([jnp.zeros_like(kept), kept], axis=0)
        if q == 0:
            block = placed
        else:
            high, low = last
            wide = mm(jnp.concatenate([a_hi, a_lo], axis=0), high)
            moved = wide[0 : 4 * no] + (wide[4 * no :] + mm(a_hi, low))
            if q % 2 == 0:
                block = jnp.concatenate([moved, placed], axis=1)
            else:
                width = moved.shape[1] - 4 * no
                tail = moved[:, width:] + placed
                block = tail if width == 0 else jnp.concatenate([moved[:, 0:width], tail], axis=1)
        width = block.shape[1]
        pmat[q, :, 0:width] = block.astype(BF16)
        if width < n_sa * rows:
            pmat[q, :, width:] = jnp.zeros((4 * no, n_sa * rows - width), BF16)
        return split(block[2 * no :])

    def send_moved():
        mine = ps.at[2 * me_tp + core]
        for k in range(1, n_tp):
            who = far(k)
            remote(pst.at[core], mine, s_p, r_p, (me_sa, who)).start()
            remote(pst.at[1 - core], mine, s_p, r_p, (sib, who)).start()
        remote(pst.at[1 - core], mine, s_p, r_p, (sib, me_tp)).start()

    def apply(left, right):
        moved = joined(*split_parts(mm(left, right), no)).astype(BF16)
        pst[0] = moved[0:rows]
        pst[1] = moved[rows:]
        send_moved()
        ps[2 * me_tp + core] = pst[core]

    def wait_pair(j):
        arrived(fall.at[2 * j : 2 * j + 2], r_f.at[j])

    def predict(begin, end, spectral):
        depth = end * rows
        left = pmat[begin:end, :, 0:depth].reshape((end - begin) * 2 * rows, depth)
        x = joined(*split_parts(mm(left, fall[0:end].reshape(depth, cols)), no))
        y2[core, begin:end] = x.astype(BF16).reshape(end - begin, rows, cols)
        if spectral:
            g = gall[begin:end].reshape((end - begin) * rows, cols).astype(F32)
            wide = jnp.concatenate([factor2] * (end - begin), axis=0)
            s2[begin * rows : depth, :] = spectral_packed(x, g, wide).astype(BF16)

    groups = min(4, n_sa // 2)
    pairs = n_sa // 2 // groups
    unit = 2 * pairs
    group = lax.div(pair, pairs)
    last = None
    for n in range(groups):
        for q in range(n * unit, (n + 1) * unit):
            last = grow(q, last)

        @pl.when(group == n)
        def _():
            arrived(gall.at[0 : n_sa - 1], r_g)
            arrived(fall.at[sib], r_f.at[pair])
            for j in range((n + 1) * pairs):
                pl.when(pair != j)(functools.partial(wait_pair, j))
            for m in range(0, n + 1, 2):
                predict(m * unit, min(m + 2, n + 1) * unit, True)
            depth = (n + 1) * unit * rows
            apply(pmat[pl.ds(2 * pair, 2), :, 0:depth].reshape(4 * rows, depth), s2[0:depth])

    for n in range(groups - 1):

        @pl.when(group == n)
        def _():
            for j in range((n + 1) * pairs, n_sa // 2):
                wait_pair(j)
            for m in range(n + 1, groups, 2):
                predict(m * unit, min(m + 2, groups) * unit, False)

    remote(y2.at[core], y2.at[core], s_y, r_y, (sib, me_tp)).start()
    first_rows = jnp.concatenate([hist[h, 0, 0:no] for h in range(2)], axis=1).astype(F32)
    q_left = pmat[me_sa][:, 0:no]
    q_own = mm(q_left, begin(dall.at[0], first_rows).astype(BF16))
    q_own = joined_halves(*split_parts(q_own, no))

    arrived(y2.at[1 - core], r_y)
    for h in range(2):
        y = y2[h]
        turned = signed(swap(y.reshape(n_sa * rows, cols).astype(F32))).astype(BF16)
        yst[:, 0:rows, h * cols : (h + 1) * cols] = y
        yst[:, rows:, h * cols : (h + 1) * cols] = turned.reshape(n_sa, rows, cols)
    base = 0.5 * (jnp.concatenate([y2[0, me_sa], y2[1, me_sa]], axis=1).astype(F32) + q_own)

    arrived(ps.at[0 : 2 * n_tp - 1], r_p)
    left = jnp.concatenate([ps[n] for n in range(2 * n_tp)], axis=1)
    final = base + (0.5 * scale) * mm(left, yst[...].reshape(2 * n_sa * rows, 2 * cols))
    f0, f1 = final[:, 0:cols], final[:, cols:]
    low = low_lanes(f0)
    out[0] = jnp.where(low, f0, swap(f1)).reshape(win.shape[2], no, cols)
    out[1] = jnp.where(low, swap(f0), f1).reshape(win.shape[2], no, cols)
    left_here(spec1.at[0 : n_tp - 1], s_s)
    left_here(dall.at[0 : n_sa - 1, 0:1], s_d)
    for send in (s_h, s_k, s_g, s_f):
        left_here(gall.at[0 : n_sa - 1], send)
    left_here(ps.at[0 : 2 * n_tp - 1], s_p)
    left_here(y2.at[core], s_y)


def shards(window, damping, propagator, coupling):
    n_sa, n_tp = lax.axis_size("sa"), lax.axis_size("tp")
    no = coupling.shape[0]
    block = window.shape[2]
    cols = window.shape[4]
    rows = block * no
    scale = 1.0 / (block * n_sa * math.sqrt(no))
    dma = lambda n: pltpu.SemaphoreType.DMA((n,))
    vm = pl.BlockSpec(memory_space=pltpu.VMEM)
    one = pltpu.SemaphoreType.DMA
    sems = [
        one, one, one, dma(n_sa // 2), one, one, one, one,
        one, one, one, dma(n_sa // 2), one, one, one, one,
    ]
    return pl.pallas_call(
        functools.partial(kernel, n_sa, n_tp, scale),
        out_shape=pltpu.VMEM((2, block, no, cols), F32),
        in_specs=[pl.BlockSpec(memory_space=pl.ANY)] * 4,
        out_specs=vm,
        scratch_shapes=[
            pltpu.VMEM(window.shape, F32),
            pltpu.VMEM(damping.shape, F32),
            pltpu.VMEM(propagator.shape, F32),
            pltpu.VMEM((1, no), F32),
            dma(4),
            pltpu.VMEM((n_sa, 8, 128), F32),
            pltpu.VMEM((2, n_sa, rows, cols), BF16),
            pltpu.VMEM((n_tp, 2 * rows, cols), BF16),
            pltpu.VMEM((2, rows, cols), BF16),
            pltpu.VMEM((n_sa, rows, cols), BF16),
            pltpu.VMEM((2, rows, cols), BF16),
            pltpu.VMEM((n_sa, rows, cols), BF16),
            pltpu.VMEM((n_sa, 2 * rows, n_sa * rows), BF16),
            pltpu.VMEM((n_sa * rows, cols), BF16),
            pltpu.VMEM((2, rows, cols), BF16),
            pltpu.VMEM((2 * n_tp, rows, cols), BF16),
            pltpu.VMEM((2, n_sa, rows, cols), BF16),
            pltpu.VMEM((n_sa, 2 * rows, 2 * cols), BF16),
        ] + sems,
        compiler_params=pltpu.CompilerParams(collective_id=0, has_side_effects=True),
        name="kadanoff",
    )(window, damping, propagator, coupling.reshape(1, no))


def solution(mesh):
    return jax.shard_map(
        shards,
        mesh=mesh,
        in_specs=(P(None, None, "sa", None, "tp"), P("sa", None), P(), P()),
        out_specs=P(None, "sa", None, "tp"),
        check_vma=False,
    )
```

```python
import functools
import math

import jax
import jax.numpy as jnp
from jax import lax
from jax.experimental import pallas as pl
from jax.experimental.pallas import tpu as pltpu
from jax.sharding import PartitionSpec as P

MESH = pl.DeviceIdType.MESH
F32 = jnp.float32
BF16 = jnp.bfloat16


def exact(a, b):
    return jnp.dot(a, b, precision=lax.Precision.HIGHEST, preferred_element_type=F32)


def split(x):
    high = x.astype(BF16)
    return high, (x - high.astype(F32)).astype(BF16)


def mm(a, b):
    return jnp.dot(a, b, preferred_element_type=F32)


def mm3(a, b):
    return mm(a[0], b[0]) + (mm(a[0], b[1]) + mm(a[1], b[0]))


def spectral_of(x_re, x_im, g_re, g_im, factor):
    lsquare_re = x_re * x_re - x_im * x_im
    lsquare_im = 2.0 * x_re * x_im
    gsquare_re = g_re * g_re - g_im * g_im
    gsquare_im = 2.0 * g_re * g_im
    sless_re = -factor * (lsquare_re * g_re + lsquare_im * g_im)
    sless_im = -factor * (lsquare_im * g_re - lsquare_re * g_im)
    sgreat_re = -factor * (gsquare_re * x_re + gsquare_im * x_im)
    sgreat_im = -factor * (gsquare_im * x_re - gsquare_re * x_im)
    return jnp.concatenate([sgreat_re - sless_re, sgreat_im - sless_im], axis=0).astype(BF16)


def low_lanes(x):
    return lax.broadcasted_iota(jnp.int32, x.shape, 1) < x.shape[1] // 2


def swap(x):
    return pltpu.roll(x, x.shape[1] // 2, 1)


def signed(x):
    return jnp.where(low_lanes(x), -x, x)


def pack(re, im):
    low = low_lanes(re)
    return jnp.where(low, re, swap(im)), jnp.where(low, swap(re), im)


def joined(a, b):
    return a + signed(swap(b))


def split_parts(x, no):
    n = x.shape[0] // (2 * no)
    y = x.reshape(n, 2, no, x.shape[1])
    return y[:, 0].reshape(n * no, x.shape[1]), y[:, 1].reshape(n * no, x.shape[1])


def spectral_packed(x, g, factor):
    low = low_lanes(x)
    xs, gs = swap(x), swap(g)
    x_re, x_im = jnp.where(low, x, xs), jnp.where(low, xs, x)
    g_re, g_im = jnp.where(low, g, gs), jnp.where(low, gs, g)
    z = x * g_re - signed(xs * g_im)
    return factor * (z * (x_re + signed(g_re)) + swap(z) * (signed(x_im) - g_im))


def kernel(
    n_sa, n_tp, scale,
    win_in, damp_in, prop_in, coup_in, out,
    win, damp, prop, coup, s_in, dall, hist, spec1, gst, gall, fst, fall, pmat, pst, ps, y2, yst,
    s_d, r_d, s_h, r_h, r_k, r_g, s_s, r_s, r_f, s_p, r_p, s_y, r_y,
):
    me_sa = lax.axis_index("sa")
    me_tp = lax.axis_index("tp")
    no = prop.shape[1]
    cols = win.shape[4]
    rows = win.shape[2] * no
    core = lax.rem(me_sa, 2)
    pair = lax.div(me_sa, 2)
    sib = pair * 2 + 1 - core

    barrier = pltpu.get_barrier_semaphore()
    def far(k):
        down = n_tp - k - (me_tp >= n_tp - k).astype(jnp.int32)
        up = k - 1 + (me_tp <= k - 1).astype(jnp.int32)
        return jnp.where(2 * me_tp < n_tp, down, up)

    def greet(sa, tp):
        pl.semaphore_signal(barrier, inc=1, device_id=(sa, tp), device_id_type=MESH)

    for k in range(1, n_tp):
        greet(me_sa, far(k))
    for k in range(1, n_sa):
        greet(lax.rem(me_sa + k, n_sa), me_tp)
    for k in range(1, n_tp):
        greet(sib, far(k))

    loads = [
        pltpu.make_async_copy(src, dst, s_in.at[n])
        for n, (src, dst) in enumerate(
            [(win_in, win), (coup_in, coup), (damp_in, damp), (prop_in, prop)]
        )
    ]
    for load in loads:
        load.start()

    def remote(src, dst, send, recv, dev):
        return pltpu.make_async_remote_copy(
            src_ref=src, dst_ref=dst, send_sem=send, recv_sem=recv,
            device_id=dev, device_id_type=MESH,
        )

    def arrived(block, recv):
        remote(block, block, s_y, recv, (sib, me_tp)).wait_recv()

    def left_here(block, send):
        remote(block, block, send, r_y, (sib, me_tp)).wait_send()

    def send_half(src, dst, send, recv):
        for k in range(1, n_sa):
            who = lax.rem(me_sa + k, n_sa)
            remote(src(lax.rem(who, 2)), dst(lax.rem(who, 2)), send, recv, (who, me_tp)).start()

    def hand_on(block):
        remote(block, block, s_h, r_k, (sib, me_tp)).start()

    for load in loads:
        load.wait()

    row_id = lax.broadcasted_iota(jnp.int32, (no, cols), 0)
    lane_id = lax.broadcasted_iota(jnp.int32, (no, cols), 1)
    tiled = (lax.rem(lane_id, no) == row_id).astype(F32)
    c_row = coup[...]
    c_lanes = exact(c_row, tiled)
    eye = lax.broadcasted_iota(jnp.int32, (no, no), 0) == lax.broadcasted_iota(jnp.int32, (no, no), 1)
    c_col = jnp.sum(jnp.where(eye, jnp.broadcast_to(c_row, (no, no)), 0.0), axis=1, keepdims=True)
    factor = c_col * c_lanes
    factor2 = jnp.concatenate([factor] * win.shape[2], axis=0)

    l_re = win[0, 0].reshape(rows, cols)
    l_im = win[0, 1].reshape(rows, cols)
    g_re = win[1, 0].reshape(rows, cols)
    g_im = win[1, 1].reshape(rows, cols)
    spec1[me_tp] = spectral_of(l_re, l_im, g_re, g_im, factor2)
    l0, l1 = pack(l_re, l_im)
    hist[0, me_sa] = l0.astype(BF16)
    hist[1, me_sa] = l1.astype(BF16)
    dmine = dall.at[me_sa]
    dmine[...] = jnp.zeros(dmine.shape, F32)
    dmine[0:1, 0:no] = damp[0:1, :]
    dmine[0:1, no : 2 * no] = damp[1:2, :]
    g0, g1 = pack(g_re, g_im)
    gst[0] = g0.astype(BF16)
    gst[1] = g1.astype(BF16)
    gall[me_sa] = gst[core]

    pl.semaphore_wait(barrier, n_sa - 1 + 2 * (n_tp - 1))
    for k in range(1, n_tp):
        who = far(k)
        remote(spec1.at[me_tp], spec1.at[me_tp], s_s, r_s, (me_sa, who)).start()
    own_half = lambda half: hist.at[half, me_sa]
    send_half(own_half, own_half, s_h, r_h.at[pair])
    hand_on(hist.at[core, me_sa])
    for k in range(1, n_sa):
        who = lax.rem(me_sa + k, n_sa)
        remote(dall.at[me_sa, 0:1], dall.at[me_sa, 0:1], s_d, r_d, (who, me_tp)).start()
    send_half(lambda half: gst.at[half], lambda half: gall.at[me_sa], s_h, r_g)

    first = (lax.broadcasted_iota(jnp.int32, (no, 2 * no), 0)
             == lax.broadcasted_iota(jnp.int32, (no, 2 * no), 1)).astype(F32)
    second = (lax.broadcasted_iota(jnp.int32, (no, 2 * no), 0) + no
              == lax.broadcasted_iota(jnp.int32, (no, 2 * no), 1)).astype(F32)
    twice = (lax.rem(lax.broadcasted_iota(jnp.int32, (no, 4 * no), 1), 2 * no)
             == lax.broadcasted_iota(jnp.int32, (no, 4 * no), 0)).astype(F32)
    u_re, u_im = prop[0], prop[1]
    u_real = jnp.concatenate(
        [exact(u_re, first) - exact(u_im, second), exact(u_im, first) + exact(u_re, second)], axis=0
    )
    u_twice = jnp.concatenate([exact(u_re, twice), exact(u_im, twice)], axis=0)
    orbital = lax.rem(lax.broadcasted_iota(jnp.int32, (2 * no, 128), 0), no)
    column = lax.broadcasted_iota(jnp.int32, (2 * no, 128), 1)

    def damping_col(ref, n):
        wide = jnp.broadcast_to(ref[0:1, :], (2 * no, 128))
        return jnp.sum(jnp.where(column == orbital + n * no, wide, 0.0), axis=1, keepdims=True)

    def begin(ref, l_packed):
        a0 = damping_col(ref, 0) * u_real
        prod = mm3(split(a0[:, 0:no]), split(l_packed))
        return joined_halves(prod[0:no], prod[no:])

    def joined_halves(a, b):
        return jnp.concatenate(
            [joined(a[:, 0:cols], b[:, 0:cols]), joined(a[:, cols:], b[:, cols:])], axis=1
        )

    start = begin(dmine, jnp.concatenate([l0[0:no], l1[0:no]], axis=1))
    start = jnp.where(me_sa == 0, start, jnp.zeros_like(start))
    start = jnp.concatenate([start, jnp.zeros((rows - no, 2 * cols), F32)], axis=0)

    for k in range(1, n_sa // 2):
        other = lax.rem(pair + k, n_sa // 2)
        both = hist.at[core, pl.ds(2 * other, 2)]
        arrived(both, r_h.at[other])
        hand_on(both)
    arrived(hist.at[core, sib], r_h.at[pair])
    arrived(hist.at[1 - core, 0 : n_sa - 1], r_k)
    arrived(spec1.at[0 : n_tp - 1], r_s)
    history = jnp.concatenate([hist[h].reshape(n_sa * rows, cols) for h in range(2)], axis=1)
    acc = None
    for c in range(n_tp):
        part = mm(spec1[c], history[c * cols : (c + 1) * cols, :])
        acc = part if acc is None else acc + part
    force = scale * joined_halves(acc[0:rows], acc[rows:]) + start
    fst[0] = force[:, 0:cols].astype(BF16)
    fst[1] = force[:, cols:].astype(BF16)
    send_half(lambda half: fst.at[half], lambda half: fall.at[me_sa], s_h, r_f.at[pair])
    fall[me_sa] = fst[core]

    arrived(dall.at[0 : n_sa - 1, 0:1], r_d)
    ops = []
    for q in range(n_sa):
        d_odd = damping_col(dall.at[q], 1)
        even = damping_col(dall.at[q], 0) * u_real
        both = exact(d_odd * u_real, even)
        ops.append((split(jnp.concatenate([even, both], axis=0)), d_odd * u_twice))

    lane = lax.broadcasted_iota(jnp.int32, (4 * no, 4 * no), 1)
    line = lax.broadcasted_iota(jnp.int32, (4 * no, 4 * no), 0)
    here = jnp.where(line < 2 * no, line, line - no)
    unit_rows = jnp.logical_or(line < no, jnp.logical_and(line >= 2 * no, line < 3 * no))
    def grow(q, last):
        (a_hi, a_lo), odd_cols = ops[q]
        at = (q % 2) * 2 * no
        placed = jnp.where(jnp.logical_and(unit_rows, lane == here + at), 1.0, 0.0)
        span = lax.broadcasted_iota(jnp.int32, (2 * no, 4 * no), 1)
        kept = jnp.where(jnp.logical_and(span >= at, span < at + no), odd_cols, 0.0)
        placed = placed + jnp.concatenate([jnp.zeros_like(kept), kept], axis=0)
        if q == 0:
            block = placed
        else:
            high, low = last
            wide = mm(jnp.concatenate([a_hi, a_lo], axis=0), high)
            moved = wide[0 : 4 * no] + (wide[4 * no :] + mm(a_hi, low))
            if q % 2 == 0:
                block = jnp.concatenate([moved, placed], axis=1)
            else:
                width = moved.shape[1] - 4 * no
                tail = moved[:, width:] + placed
                block = tail if width == 0 else jnp.concatenate([moved[:, 0:width], tail], axis=1)
        width = block.shape[1]
        pmat[q, :, 0:width] = block.astype(BF16)
        if width < n_sa * rows:
            pmat[q, :, width:] = jnp.zeros((4 * no, n_sa * rows - width), BF16)
        return split(block[2 * no :])

    def send_moved():
        mine = ps.at[2 * me_tp + core]
        for k in range(1, n_tp):
            who = far(k)
            remote(pst.at[core], mine, s_p, r_p, (me_sa, who)).start()
            remote(pst.at[1 - core], mine, s_p, r_p, (sib, who)).start()
        remote(pst.at[1 - core], mine, s_p, r_p, (sib, me_tp)).start()

    def apply(left, right):
        moved = joined(*split_parts(mm(left, right), no)).astype(BF16)
        pst[0] = moved[0:rows]
        pst[1] = moved[rows:]
        send_moved()
        ps[2 * me_tp + core] = pst[core]

    def wait_pair(j):
        arrived(fall.at[2 * j : 2 * j + 2], r_f.at[j])

    def predict(begin, end):
        depth = end * rows
        left = pmat[begin:end, :, 0:depth].reshape((end - begin) * 2 * rows, depth)
        return joined(*split_parts(mm(left, fall[0:end].reshape(depth, cols)), no))

    def keep(x, begin, end):
        y2[core, begin:end] = x.astype(BF16).reshape(end - begin, rows, cols)

    wide = jnp.concatenate([factor2] * (n_sa // min(4, n_sa // 2)), axis=0)

    def spectral(x, begin, end):
        g = gall[begin:end].reshape((end - begin) * rows, cols).astype(F32)
        return spectral_packed(x, g, wide).astype(BF16)

    groups = min(4, n_sa // 2)
    pairs = n_sa // 2 // groups
    unit = 2 * pairs
    group = lax.div(pair, pairs)
    last = None
    for n in range(groups):
        for q in range(n * unit, (n + 1) * unit):
            last = grow(q, last)

        @pl.when(group == n)
        def _():
            arrived(gall.at[0 : n_sa - 1], r_g)
            arrived(fall.at[sib], r_f.at[pair])
            for j in range((n + 1) * pairs):
                pl.when(pair != j)(functools.partial(wait_pair, j))
            spans = [(m * unit, (m + 1) * unit) for m in range(n + 1)]
            tiles = [predict(*span) for span in spans]
            right = jnp.concatenate([spectral(x, *span) for x, span in zip(tiles, spans)], axis=0)
            apply(pmat[pl.ds(2 * pair, 2), :, 0 : right.shape[0]].reshape(4 * rows, -1), right)
            for x, span in zip(tiles, spans):
                keep(x, *span)

    for n in range(groups - 1):

        @pl.when(group == n)
        def _():
            for j in range((n + 1) * pairs, n_sa // 2):
                wait_pair(j)
            for m in range(n + 1, groups):
                span = (m * unit, (m + 1) * unit)
                keep(predict(*span), *span)

    remote(y2.at[core], y2.at[core], s_y, r_y, (sib, me_tp)).start()
    first_rows = jnp.concatenate([hist[h, 0, 0:no] for h in range(2)], axis=1).astype(F32)
    q_left = pmat[me_sa][:, 0:no]
    q_own = mm(q_left, begin(dall.at[0], first_rows).astype(BF16))
    q_own = joined_halves(*split_parts(q_own, no))

    arrived(y2.at[1 - core], r_y)
    for h in range(2):
        y = y2[h]
        turned = signed(swap(y.reshape(n_sa * rows, cols).astype(F32))).astype(BF16)
        yst[:, 0:rows, h * cols : (h + 1) * cols] = y
        yst[:, rows:, h * cols : (h + 1) * cols] = turned.reshape(n_sa, rows, cols)
    base = 0.5 * (jnp.concatenate([y2[0, me_sa], y2[1, me_sa]], axis=1).astype(F32) + q_own)

    arrived(ps.at[0 : 2 * n_tp - 1], r_p)
    left = jnp.concatenate([ps[n] for n in range(2 * n_tp)], axis=1)
    final = base + (0.5 * scale) * mm(left, yst[...].reshape(2 * n_sa * rows, 2 * cols))
    f0, f1 = final[:, 0:cols], final[:, cols:]
    low = low_lanes(f0)
    out[0] = jnp.where(low, f0, swap(f1)).reshape(win.shape[2], no, cols)
    out[1] = jnp.where(low, swap(f0), f1).reshape(win.shape[2], no, cols)
    left_here(spec1.at[0 : n_tp - 1], s_s)
    left_here(dall.at[0 : n_sa - 1, 0:1], s_d)
    left_here(yst.at[0 : n_sa - 1], s_h)
    left_here(ps.at[0 : 2 * n_tp - 1], s_p)
    left_here(y2.at[core], s_y)


def shards(window, damping, propagator, coupling):
    n_sa, n_tp = lax.axis_size("sa"), lax.axis_size("tp")
    no = coupling.shape[0]
    block = window.shape[2]
    cols = window.shape[4]
    rows = block * no
    scale = 1.0 / (block * n_sa * math.sqrt(no))
    dma = lambda n: pltpu.SemaphoreType.DMA((n,))
    vm = pl.BlockSpec(memory_space=pltpu.VMEM)
    one = pltpu.SemaphoreType.DMA
    sems = [
        one, one, one, dma(n_sa // 2), one, one,
        one, one, dma(n_sa // 2), one, one, one, one,
    ]
    return pl.pallas_call(
        functools.partial(kernel, n_sa, n_tp, scale),
        out_shape=pltpu.VMEM((2, block, no, cols), F32),
        in_specs=[pl.BlockSpec(memory_space=pl.ANY)] * 4,
        out_specs=vm,
        scratch_shapes=[
            pltpu.VMEM(window.shape, F32),
            pltpu.VMEM(damping.shape, F32),
            pltpu.VMEM(propagator.shape, F32),
            pltpu.VMEM((1, no), F32),
            dma(4),
            pltpu.VMEM((n_sa, 8, 128), F32),
            pltpu.VMEM((2, n_sa, rows, cols), BF16),
            pltpu.VMEM((n_tp, 2 * rows, cols), BF16),
            pltpu.VMEM((2, rows, cols), BF16),
            pltpu.VMEM((n_sa, rows, cols), BF16),
            pltpu.VMEM((2, rows, cols), BF16),
            pltpu.VMEM((n_sa, rows, cols), BF16),
            pltpu.VMEM((n_sa, 2 * rows, n_sa * rows), BF16),
            pltpu.VMEM((2, rows, cols), BF16),
            pltpu.VMEM((2 * n_tp, rows, cols), BF16),
            pltpu.VMEM((2, n_sa, rows, cols), BF16),
            pltpu.VMEM((n_sa, 2 * rows, 2 * cols), BF16),
        ] + sems,
        compiler_params=pltpu.CompilerParams(collective_id=0, has_side_effects=True),
        name="kadanoff",
    )(window, damping, propagator, coupling.reshape(1, no))


def solution(mesh):
    return jax.shard_map(
        shards,
        mesh=mesh,
        in_specs=(P(None, None, "sa", None, "tp"), P("sa", None), P(), P()),
        out_specs=P(None, "sa", None, "tp"),
        check_vma=False,
    )
```

```python
import functools
import math

import jax
import jax.numpy as jnp
from jax import lax
from jax.experimental import pallas as pl
from jax.experimental.pallas import tpu as pltpu
from jax.sharding import PartitionSpec as P

MESH = pl.DeviceIdType.MESH
F32 = jnp.float32
BF16 = jnp.bfloat16


def exact(a, b):
    return jnp.dot(a, b, precision=lax.Precision.HIGHEST, preferred_element_type=F32)


def split(x):
    high = x.astype(BF16)
    return high, (x - high.astype(F32)).astype(BF16)


def mm(a, b):
    return jnp.dot(a, b, preferred_element_type=F32)


def mm3(a, b):
    return mm(a[0], b[0]) + (mm(a[0], b[1]) + mm(a[1], b[0]))


def spectral_of(x_re, x_im, g_re, g_im, factor):
    lsquare_re = x_re * x_re - x_im * x_im
    lsquare_im = 2.0 * x_re * x_im
    gsquare_re = g_re * g_re - g_im * g_im
    gsquare_im = 2.0 * g_re * g_im
    sless_re = -factor * (lsquare_re * g_re + lsquare_im * g_im)
    sless_im = -factor * (lsquare_im * g_re - lsquare_re * g_im)
    sgreat_re = -factor * (gsquare_re * x_re + gsquare_im * x_im)
    sgreat_im = -factor * (gsquare_im * x_re - gsquare_re * x_im)
    return jnp.concatenate([sgreat_re - sless_re, sgreat_im - sless_im], axis=0).astype(BF16)


def low_lanes(x):
    return lax.broadcasted_iota(jnp.int32, x.shape, 1) < x.shape[1] // 2


def swap(x):
    return pltpu.roll(x, x.shape[1] // 2, 1)


def signed(x):
    return jnp.where(low_lanes(x), -x, x)


def pack(re, im):
    low = low_lanes(re)
    return jnp.where(low, re, swap(im)), jnp.where(low, swap(re), im)


def joined(a, b):
    return a + signed(swap(b))


def split_parts(x, no):
    n = x.shape[0] // (2 * no)
    y = x.reshape(n, 2, no, x.shape[1])
    return y[:, 0].reshape(n * no, x.shape[1]), y[:, 1].reshape(n * no, x.shape[1])


def spectral_packed(x, g, factor):
    low = low_lanes(x)
    xs, gs = swap(x), swap(g)
    x_re, x_im = jnp.where(low, x, xs), jnp.where(low, xs, x)
    g_re, g_im = jnp.where(low, g, gs), jnp.where(low, gs, g)
    z = x * g_re - signed(xs * g_im)
    return factor * (z * (x_re + signed(g_re)) + swap(z) * (signed(x_im) - g_im))


def kernel(
    n_sa, n_tp, scale,
    win_in, damp_in, prop_in, coup_in, out,
    win, damp, prop, coup, s_in, dall, hist, spec1, gst, gall, fst, fall, pmat, pst, ps, y2, yst,
    s_d, r_d, s_h, r_h, r_k, r_g, s_s, r_s, r_f, s_p, r_p, s_y, r_y,
):
    me_sa = lax.axis_index("sa")
    me_tp = lax.axis_index("tp")
    no = prop.shape[1]
    cols = win.shape[4]
    rows = win.shape[2] * no
    core = lax.rem(me_sa, 2)
    pair = lax.div(me_sa, 2)
    sib = pair * 2 + 1 - core

    barrier = pltpu.get_barrier_semaphore()
    def far(k):
        down = n_tp - k - (me_tp >= n_tp - k).astype(jnp.int32)
        up = k - 1 + (me_tp <= k - 1).astype(jnp.int32)
        return jnp.where(2 * me_tp < n_tp, down, up)

    def greet(sa, tp):
        pl.semaphore_signal(barrier, inc=1, device_id=(sa, tp), device_id_type=MESH)

    for k in range(1, n_tp):
        greet(me_sa, far(k))
    for k in range(1, n_sa):
        greet(lax.rem(me_sa + k, n_sa), me_tp)
    for k in range(1, n_tp):
        greet(sib, far(k))

    loads = [
        pltpu.make_async_copy(src, dst, s_in.at[n])
        for n, (src, dst) in enumerate(
            [(win_in, win), (coup_in, coup), (damp_in, damp), (prop_in, prop)]
        )
    ]
    for load in loads:
        load.start()

    def remote(src, dst, send, recv, dev):
        return pltpu.make_async_remote_copy(
            src_ref=src, dst_ref=dst, send_sem=send, recv_sem=recv,
            device_id=dev, device_id_type=MESH,
        )

    def arrived(block, recv):
        remote(block, block, s_y, recv, (sib, me_tp)).wait_recv()

    def left_here(block, send):
        remote(block, block, send, r_y, (sib, me_tp)).wait_send()

    def send_half(src, dst, send, recv):
        for k in range(1, n_sa):
            who = lax.rem(me_sa + k, n_sa)
            remote(src(lax.rem(who, 2)), dst(lax.rem(who, 2)), send, recv, (who, me_tp)).start()

    def hand_on(block):
        remote(block, block, s_h, r_k, (sib, me_tp)).start()

    for load in loads:
        load.wait()

    row_id = lax.broadcasted_iota(jnp.int32, (no, cols), 0)
    lane_id = lax.broadcasted_iota(jnp.int32, (no, cols), 1)
    tiled = (lax.rem(lane_id, no) == row_id).astype(F32)
    c_row = coup[...]
    c_lanes = exact(c_row, tiled)
    eye = lax.broadcasted_iota(jnp.int32, (no, no), 0) == lax.broadcasted_iota(jnp.int32, (no, no), 1)
    c_col = jnp.sum(jnp.where(eye, jnp.broadcast_to(c_row, (no, no)), 0.0), axis=1, keepdims=True)
    factor = c_col * c_lanes
    factor2 = jnp.concatenate([factor] * win.shape[2], axis=0)

    l_re = win[0, 0].reshape(rows, cols)
    l_im = win[0, 1].reshape(rows, cols)
    g_re = win[1, 0].reshape(rows, cols)
    g_im = win[1, 1].reshape(rows, cols)
    spec1[me_tp] = spectral_of(l_re, l_im, g_re, g_im, factor2)
    l0, l1 = pack(l_re, l_im)
    hist[0, me_sa] = l0.astype(BF16)
    hist[1, me_sa] = l1.astype(BF16)
    dmine = dall.at[me_sa]
    dmine[...] = jnp.zeros(dmine.shape, F32)
    dmine[0:1, 0:no] = damp[0:1, :]
    dmine[0:1, no : 2 * no] = damp[1:2, :]
    g0, g1 = pack(g_re, g_im)
    gst[0] = g0.astype(BF16)
    gst[1] = g1.astype(BF16)
    gall[me_sa] = gst[core]

    pl.semaphore_wait(barrier, n_sa - 1 + 2 * (n_tp - 1))
    for k in range(1, n_tp):
        who = far(k)
        remote(spec1.at[me_tp], spec1.at[me_tp], s_s, r_s, (me_sa, who)).start()
    own_half = lambda half: hist.at[half, me_sa]
    send_half(own_half, own_half, s_h, r_h.at[pair])
    hand_on(hist.at[core, me_sa])
    for k in range(1, n_sa):
        who = lax.rem(me_sa + k, n_sa)
        remote(dall.at[me_sa, 0:1], dall.at[me_sa, 0:1], s_d, r_d, (who, me_tp)).start()
    send_half(lambda half: gst.at[half], lambda half: gall.at[me_sa], s_h, r_g)

    first = (lax.broadcasted_iota(jnp.int32, (no, 2 * no), 0)
             == lax.broadcasted_iota(jnp.int32, (no, 2 * no), 1)).astype(F32)
    second = (lax.broadcasted_iota(jnp.int32, (no, 2 * no), 0) + no
              == lax.broadcasted_iota(jnp.int32, (no, 2 * no), 1)).astype(F32)
    twice = (lax.rem(lax.broadcasted_iota(jnp.int32, (no, 4 * no), 1), 2 * no)
             == lax.broadcasted_iota(jnp.int32, (no, 4 * no), 0)).astype(F32)
    u_re, u_im = prop[0], prop[1]
    u_real = jnp.concatenate(
        [exact(u_re, first) - exact(u_im, second), exact(u_im, first) + exact(u_re, second)], axis=0
    )
    u_twice = jnp.concatenate([exact(u_re, twice), exact(u_im, twice)], axis=0)
    orbital = lax.rem(lax.broadcasted_iota(jnp.int32, (2 * no, 128), 0), no)
    column = lax.broadcasted_iota(jnp.int32, (2 * no, 128), 1)

    def damping_col(ref, n):
        wide = jnp.broadcast_to(ref[0:1, :], (2 * no, 128))
        return jnp.sum(jnp.where(column == orbital + n * no, wide, 0.0), axis=1, keepdims=True)

    def begin(ref, l_packed):
        a0 = damping_col(ref, 0) * u_real
        prod = mm3(split(a0[:, 0:no]), split(l_packed))
        return joined_halves(prod[0:no], prod[no:])

    def joined_halves(a, b):
        return jnp.concatenate(
            [joined(a[:, 0:cols], b[:, 0:cols]), joined(a[:, cols:], b[:, cols:])], axis=1
        )

    start = begin(dmine, jnp.concatenate([l0[0:no], l1[0:no]], axis=1))
    start = jnp.where(me_sa == 0, start, jnp.zeros_like(start))
    start = jnp.concatenate([start, jnp.zeros((rows - no, 2 * cols), F32)], axis=0)

    for k in range(1, n_sa // 2):
        other = lax.rem(pair + k, n_sa // 2)
        both = hist.at[core, pl.ds(2 * other, 2)]
        arrived(both, r_h.at[other])
        hand_on(both)
    arrived(hist.at[core, sib], r_h.at[pair])
    arrived(hist.at[1 - core, 0 : n_sa - 1], r_k)
    arrived(spec1.at[0 : n_tp - 1], r_s)
    history = jnp.concatenate([hist[h].reshape(n_sa * rows, cols) for h in range(2)], axis=1)
    acc = None
    for c in range(n_tp):
        part = mm(spec1[c], history[c * cols : (c + 1) * cols, :])
        acc = part if acc is None else acc + part
    force = scale * joined_halves(acc[0:rows], acc[rows:]) + start
    fst[0] = force[:, 0:cols].astype(BF16)
    fst[1] = force[:, cols:].astype(BF16)
    send_half(lambda half: fst.at[half], lambda half: fall.at[me_sa], s_h, r_f.at[pair])
    fall[me_sa] = fst[core]

    arrived(dall.at[0 : n_sa - 1, 0:1], r_d)
    ops = []
    for q in range(n_sa):
        d_odd = damping_col(dall.at[q], 1)
        even = damping_col(dall.at[q], 0) * u_real
        both = exact(d_odd * u_real, even)
        ops.append((split(jnp.concatenate([even, both], axis=0)), d_odd * u_twice))

    lane = lax.broadcasted_iota(jnp.int32, (4 * no, 4 * no), 1)
    line = lax.broadcasted_iota(jnp.int32, (4 * no, 4 * no), 0)
    here = jnp.where(line < 2 * no, line, line - no)
    unit_rows = jnp.logical_or(line < no, jnp.logical_and(line >= 2 * no, line < 3 * no))
    def grow(q, last):
        (a_hi, a_lo), odd_cols = ops[q]
        at = (q % 2) * 2 * no
        placed = jnp.where(jnp.logical_and(unit_rows, lane == here + at), 1.0, 0.0)
        span = lax.broadcasted_iota(jnp.int32, (2 * no, 4 * no), 1)
        kept = jnp.where(jnp.logical_and(span >= at, span < at + no), odd_cols, 0.0)
        placed = placed + jnp.concatenate([jnp.zeros_like(kept), kept], axis=0)
        if q == 0:
            block = placed
        else:
            high, low = last
            wide = mm(jnp.concatenate([a_hi, a_lo], axis=0), high)
            moved = wide[0 : 4 * no] + (wide[4 * no :] + mm(a_hi, low))
            if q % 2 == 0:
                block = jnp.concatenate([moved, placed], axis=1)
            else:
                width = moved.shape[1] - 4 * no
                tail = moved[:, width:] + placed
                block = tail if width == 0 else jnp.concatenate([moved[:, 0:width], tail], axis=1)
        width = block.shape[1]
        pmat[q, :, 0:width] = block.astype(BF16)
        if width < n_sa * rows:
            pmat[q, :, width:] = jnp.zeros((4 * no, n_sa * rows - width), BF16)
        return split(block[2 * no :])

    def send_moved():
        mine = ps.at[2 * me_tp + core]
        for k in range(1, n_tp):
            who = far(k)
            remote(pst.at[core], mine, s_p, r_p, (me_sa, who)).start()
            remote(pst.at[1 - core], mine, s_p, r_p, (sib, who)).start()
        remote(pst.at[1 - core], mine, s_p, r_p, (sib, me_tp)).start()

    def apply(left, right):
        moved = joined(*split_parts(mm(left, right), no)).astype(BF16)
        pst[0] = moved[0:rows]
        pst[1] = moved[rows:]
        send_moved()
        ps[2 * me_tp + core] = pst[core]

    def wait_pair(j):
        arrived(fall.at[2 * j : 2 * j + 2], r_f.at[j])

    def predict(begin, end):
        depth = end * rows
        left = pmat[begin:end, :, 0:depth].reshape((end - begin) * 2 * rows, depth)
        return joined(*split_parts(mm(left, fall[0:end].reshape(depth, cols)), no))

    def keep(x, begin, end):
        y2[core, begin:end] = x.astype(BF16).reshape(end - begin, rows, cols)

    wide = jnp.concatenate([factor2] * (n_sa // min(4, n_sa // 2)), axis=0)

    def spectral(x, begin, end):
        g = gall[begin:end].reshape((end - begin) * rows, cols).astype(F32)
        return spectral_packed(x, g, wide).astype(BF16)

    groups = min(4, n_sa // 2)
    pairs = n_sa // 2 // groups
    unit = 2 * pairs
    group = lax.div(pair, pairs)
    last = None
    for n in range(groups):
        for q in range(n * unit, (n + 1) * unit):
            last = grow(q, last)

        @pl.when(group == n)
        def _():
            arrived(gall.at[0 : n_sa - 1], r_g)
            arrived(fall.at[sib], r_f.at[pair])
            for j in range((n + 1) * pairs):
                pl.when(pair != j)(functools.partial(wait_pair, j))
            spans = [(m * unit, (m + 1) * unit) for m in range(n + 1)]
            tiles = [predict(*span) for span in spans]
            right = jnp.concatenate([spectral(x, *span) for x, span in zip(tiles, spans)], axis=0)
            apply(pmat[pl.ds(2 * pair, 2), :, 0 : right.shape[0]].reshape(4 * rows, -1), right)
            for x, span in zip(tiles, spans):
                keep(x, *span)

    for n in range(groups - 1):

        @pl.when(group == n)
        def _():
            for j in range((n + 1) * pairs, n_sa // 2):
                wait_pair(j)
            for m in range(n + 1, groups):
                span = (m * unit, (m + 1) * unit)
                keep(predict(*span), *span)

    remote(y2.at[core], y2.at[core], s_y, r_y, (sib, me_tp)).start()
    first_rows = jnp.concatenate([hist[h, 0, 0:no] for h in range(2)], axis=1).astype(F32)
    q_left = pmat[me_sa][:, 0:no]
    q_own = mm(q_left, begin(dall.at[0], first_rows).astype(BF16))
    q_own = joined_halves(*split_parts(q_own, no))

    arrived(y2.at[1 - core], r_y)
    def unpack(h0, h1):
        low = low_lanes(h0)
        return jnp.where(low, h0, swap(h1)), jnp.where(low, swap(h0), h1)

    y_re, y_im = unpack(*[y2[h].reshape(n_sa * rows, cols).astype(F32) for h in range(2)])
    for at, columns in ((0, (y_re, y_im)), (rows, (-y_im, y_re))):
        for h in range(2):
            block = columns[h].astype(BF16).reshape(n_sa, rows, cols)
            yst[:, at : at + rows, h * cols : (h + 1) * cols] = block
    base = unpack(*[
        0.5 * (y2[h, me_sa].astype(F32) + q_own[:, h * cols : (h + 1) * cols]) for h in range(2)
    ])

    arrived(ps.at[0 : 2 * n_tp - 1], r_p)
    left = jnp.concatenate([ps[n] for n in range(2 * n_tp)], axis=1)
    final = (0.5 * scale) * mm(left, yst[...].reshape(2 * n_sa * rows, 2 * cols))
    for h in range(2):
        total = base[h] + final[:, h * cols : (h + 1) * cols]
        out[h] = total.reshape(win.shape[2], no, cols)
    left_here(spec1.at[0 : n_tp - 1], s_s)
    left_here(dall.at[0 : n_sa - 1, 0:1], s_d)
    left_here(yst.at[0 : n_sa - 1], s_h)
    left_here(ps.at[0 : 2 * n_tp - 1], s_p)
    left_here(y2.at[core], s_y)


def shards(window, damping, propagator, coupling):
    n_sa, n_tp = lax.axis_size("sa"), lax.axis_size("tp")
    no = coupling.shape[0]
    block = window.shape[2]
    cols = window.shape[4]
    rows = block * no
    scale = 1.0 / (block * n_sa * math.sqrt(no))
    dma = lambda n: pltpu.SemaphoreType.DMA((n,))
    vm = pl.BlockSpec(memory_space=pltpu.VMEM)
    one = pltpu.SemaphoreType.DMA
    sems = [
        one, one, one, dma(n_sa // 2), one, one,
        one, one, dma(n_sa // 2), one, one, one, one,
    ]
    return pl.pallas_call(
        functools.partial(kernel, n_sa, n_tp, scale),
        out_shape=pltpu.VMEM((2, block, no, cols), F32),
        in_specs=[pl.BlockSpec(memory_space=pl.ANY)] * 4,
        out_specs=vm,
        scratch_shapes=[
            pltpu.VMEM(window.shape, F32),
            pltpu.VMEM(damping.shape, F32),
            pltpu.VMEM(propagator.shape, F32),
            pltpu.VMEM((1, no), F32),
            dma(4),
            pltpu.VMEM((n_sa, 8, 128), F32),
            pltpu.VMEM((2, n_sa, rows, cols), BF16),
            pltpu.VMEM((n_tp, 2 * rows, cols), BF16),
            pltpu.VMEM((2, rows, cols), BF16),
            pltpu.VMEM((n_sa, rows, cols), BF16),
            pltpu.VMEM((2, rows, cols), BF16),
            pltpu.VMEM((n_sa, rows, cols), BF16),
            pltpu.VMEM((n_sa, 2 * rows, n_sa * rows), BF16),
            pltpu.VMEM((2, rows, cols), BF16),
            pltpu.VMEM((2 * n_tp, rows, cols), BF16),
            pltpu.VMEM((2, n_sa, rows, cols), BF16),
            pltpu.VMEM((n_sa, 2 * rows, 2 * cols), BF16),
        ] + sems,
        compiler_params=pltpu.CompilerParams(collective_id=0, has_side_effects=True),
        name="kadanoff",
    )(window, damping, propagator, coupling.reshape(1, no))


def solution(mesh):
    return jax.shard_map(
        shards,
        mesh=mesh,
        in_specs=(P(None, None, "sa", None, "tp"), P("sa", None), P(), P()),
        out_specs=P(None, "sa", None, "tp"),
        check_vma=False,
    )
```

```python
import functools
import math

import jax
import jax.numpy as jnp
from jax import lax
from jax.experimental import pallas as pl
from jax.experimental.pallas import tpu as pltpu
from jax.sharding import PartitionSpec as P

MESH = pl.DeviceIdType.MESH
F32 = jnp.float32
BF16 = jnp.bfloat16


def exact(a, b):
    return jnp.dot(a, b, precision=lax.Precision.HIGHEST, preferred_element_type=F32)


def split(x):
    high = x.astype(BF16)
    return high, (x - high.astype(F32)).astype(BF16)


def mm(a, b):
    return jnp.dot(a, b, preferred_element_type=F32)


def mm3(a, b):
    return mm(a[0], b[0]) + (mm(a[0], b[1]) + mm(a[1], b[0]))


def spectral_of(x_re, x_im, g_re, g_im, factor):
    lsquare_re = x_re * x_re - x_im * x_im
    lsquare_im = 2.0 * x_re * x_im
    gsquare_re = g_re * g_re - g_im * g_im
    gsquare_im = 2.0 * g_re * g_im
    sless_re = -factor * (lsquare_re * g_re + lsquare_im * g_im)
    sless_im = -factor * (lsquare_im * g_re - lsquare_re * g_im)
    sgreat_re = -factor * (gsquare_re * x_re + gsquare_im * x_im)
    sgreat_im = -factor * (gsquare_im * x_re - gsquare_re * x_im)
    return jnp.concatenate([sgreat_re - sless_re, sgreat_im - sless_im], axis=0).astype(BF16)


def low_lanes(x):
    return lax.broadcasted_iota(jnp.int32, x.shape, 1) < x.shape[1] // 2


def swap(x):
    return pltpu.roll(x, x.shape[1] // 2, 1)


def signed(x):
    return jnp.where(low_lanes(x), -x, x)


def pack(re, im):
    low = low_lanes(re)
    return jnp.where(low, re, swap(im)), jnp.where(low, swap(re), im)


def joined(a, b):
    return a + signed(swap(b))


def split_parts(x, no):
    n = x.shape[0] // (2 * no)
    y = x.reshape(n, 2, no, x.shape[1])
    return y[:, 0].reshape(n * no, x.shape[1]), y[:, 1].reshape(n * no, x.shape[1])


def spectral_packed(x, g, factor):
    low = low_lanes(x)
    xs, gs = swap(x), swap(g)
    x_re, x_im = jnp.where(low, x, xs), jnp.where(low, xs, x)
    g_re, g_im = jnp.where(low, g, gs), jnp.where(low, gs, g)
    z = x * g_re - signed(xs * g_im)
    return factor * (z * (x_re + signed(g_re)) + swap(z) * (signed(x_im) - g_im))


def kernel(
    n_sa, n_tp, scale,
    win_in, damp_in, prop_in, coup_in, out,
    win, damp, prop, coup, s_in, dall, hist, spec1, gst, gall, fst, fall, pmat, pst, ps, y2, yst,
    s_d, r_d, s_h, r_h, r_k, r_g, s_s, r_s, r_f, s_p, r_p, s_y, r_y,
):
    me_sa = lax.axis_index("sa")
    me_tp = lax.axis_index("tp")
    no = prop.shape[1]
    cols = win.shape[4]
    rows = win.shape[2] * no
    core = lax.rem(me_sa, 2)
    pair = lax.div(me_sa, 2)
    sib = pair * 2 + 1 - core

    barrier = pltpu.get_barrier_semaphore()
    def far(k):
        down = n_tp - k - (me_tp >= n_tp - k).astype(jnp.int32)
        up = k - 1 + (me_tp <= k - 1).astype(jnp.int32)
        return jnp.where(2 * me_tp < n_tp, down, up)

    def greet(sa, tp):
        pl.semaphore_signal(barrier, inc=1, device_id=(sa, tp), device_id_type=MESH)

    for k in range(1, n_tp):
        greet(me_sa, far(k))
    for k in range(1, n_sa):
        greet(lax.rem(me_sa + k, n_sa), me_tp)
    for k in range(1, n_tp):
        greet(sib, far(k))

    loads = [
        pltpu.make_async_copy(src, dst, s_in.at[n])
        for n, (src, dst) in enumerate(
            [(win_in, win), (coup_in, coup), (damp_in, damp), (prop_in, prop)]
        )
    ]
    for load in loads:
        load.start()

    def remote(src, dst, send, recv, dev):
        return pltpu.make_async_remote_copy(
            src_ref=src, dst_ref=dst, send_sem=send, recv_sem=recv,
            device_id=dev, device_id_type=MESH,
        )

    def arrived(block, recv):
        remote(block, block, s_y, recv, (sib, me_tp)).wait_recv()

    def left_here(block, send):
        remote(block, block, send, r_y, (sib, me_tp)).wait_send()

    def send_half(src, dst, send, recv):
        for k in range(1, n_sa):
            who = lax.rem(me_sa + k, n_sa)
            remote(src(lax.rem(who, 2)), dst(lax.rem(who, 2)), send, recv, (who, me_tp)).start()

    def hand_on(block):
        remote(block, block, s_h, r_k, (sib, me_tp)).start()

    for load in loads:
        load.wait()

    row_id = lax.broadcasted_iota(jnp.int32, (no, cols), 0)
    lane_id = lax.broadcasted_iota(jnp.int32, (no, cols), 1)
    tiled = (lax.rem(lane_id, no) == row_id).astype(F32)
    c_row = coup[...]
    c_lanes = exact(c_row, tiled)
    eye = lax.broadcasted_iota(jnp.int32, (no, no), 0) == lax.broadcasted_iota(jnp.int32, (no, no), 1)
    c_col = jnp.sum(jnp.where(eye, jnp.broadcast_to(c_row, (no, no)), 0.0), axis=1, keepdims=True)
    factor = c_col * c_lanes
    factor2 = jnp.concatenate([factor] * win.shape[2], axis=0)

    l_re = win[0, 0].reshape(rows, cols)
    l_im = win[0, 1].reshape(rows, cols)
    g_re = win[1, 0].reshape(rows, cols)
    g_im = win[1, 1].reshape(rows, cols)
    spec1[me_tp] = spectral_of(l_re, l_im, g_re, g_im, factor2)
    l0, l1 = pack(l_re, l_im)
    hist[0, me_sa] = l0.astype(BF16)
    hist[1, me_sa] = l1.astype(BF16)
    dmine = dall.at[me_sa]
    dmine[...] = jnp.zeros(dmine.shape, F32)
    dmine[0:1, 0:no] = damp[0:1, :]
    dmine[0:1, no : 2 * no] = damp[1:2, :]
    g0, g1 = pack(g_re, g_im)
    gst[0] = g0.astype(BF16)
    gst[1] = g1.astype(BF16)
    gall[me_sa] = gst[core]

    pl.semaphore_wait(barrier, n_sa - 1 + 2 * (n_tp - 1))
    for k in range(1, n_tp):
        who = far(k)
        remote(spec1.at[me_tp], spec1.at[me_tp], s_s, r_s, (me_sa, who)).start()
    own_half = lambda half: hist.at[half, me_sa]
    send_half(own_half, own_half, s_h, r_h.at[pair])
    hand_on(hist.at[core, me_sa])
    for k in range(1, n_sa):
        who = lax.rem(me_sa + k, n_sa)
        remote(dall.at[me_sa, 0:1], dall.at[me_sa, 0:1], s_d, r_d, (who, me_tp)).start()
    send_half(lambda half: gst.at[half], lambda half: gall.at[me_sa], s_h, r_g)

    first = (lax.broadcasted_iota(jnp.int32, (no, 2 * no), 0)
             == lax.broadcasted_iota(jnp.int32, (no, 2 * no), 1)).astype(F32)
    second = (lax.broadcasted_iota(jnp.int32, (no, 2 * no), 0) + no
              == lax.broadcasted_iota(jnp.int32, (no, 2 * no), 1)).astype(F32)
    twice = (lax.rem(lax.broadcasted_iota(jnp.int32, (no, 4 * no), 1), 2 * no)
             == lax.broadcasted_iota(jnp.int32, (no, 4 * no), 0)).astype(F32)
    u_re, u_im = prop[0], prop[1]
    u_real = jnp.concatenate(
        [exact(u_re, first) - exact(u_im, second), exact(u_im, first) + exact(u_re, second)], axis=0
    )
    u_twice = jnp.concatenate([exact(u_re, twice), exact(u_im, twice)], axis=0)
    orbital = lax.rem(lax.broadcasted_iota(jnp.int32, (2 * no, 128), 0), no)
    column = lax.broadcasted_iota(jnp.int32, (2 * no, 128), 1)

    def damping_col(ref, n):
        wide = jnp.broadcast_to(ref[0:1, :], (2 * no, 128))
        return jnp.sum(jnp.where(column == orbital + n * no, wide, 0.0), axis=1, keepdims=True)

    def begin(ref, l_packed):
        a0 = damping_col(ref, 0) * u_real
        prod = mm3(split(a0[:, 0:no]), split(l_packed))
        return joined_halves(prod[0:no], prod[no:])

    def joined_halves(a, b):
        return jnp.concatenate(
            [joined(a[:, 0:cols], b[:, 0:cols]), joined(a[:, cols:], b[:, cols:])], axis=1
        )

    start = begin(dmine, jnp.concatenate([l0[0:no], l1[0:no]], axis=1))
    start = jnp.where(me_sa == 0, start, jnp.zeros_like(start))
    start = jnp.concatenate([start, jnp.zeros((rows - no, 2 * cols), F32)], axis=0)

    for k in range(1, n_sa // 2):
        other = lax.rem(pair + k, n_sa // 2)
        both = hist.at[core, pl.ds(2 * other, 2)]
        arrived(both, r_h.at[other])
        hand_on(both)
    arrived(hist.at[core, sib], r_h.at[pair])
    arrived(hist.at[1 - core, 0 : n_sa - 1], r_k)
    arrived(spec1.at[0 : n_tp - 1], r_s)
    history = jnp.concatenate([hist[h].reshape(n_sa * rows, cols) for h in range(2)], axis=1)
    acc = None
    for c in range(n_tp):
        part = mm(spec1[c], history[c * cols : (c + 1) * cols, :])
        acc = part if acc is None else acc + part
    force = scale * joined_halves(acc[0:rows], acc[rows:]) + start
    fst[0] = force[:, 0:cols].astype(BF16)
    fst[1] = force[:, cols:].astype(BF16)
    send_half(lambda half: fst.at[half], lambda half: fall.at[me_sa], s_h, r_f.at[pair])
    fall[me_sa] = fst[core]

    arrived(dall.at[0 : n_sa - 1, 0:1], r_d)
    ops = []
    for q in range(n_sa):
        d_odd = damping_col(dall.at[q], 1)
        even = damping_col(dall.at[q], 0) * u_real
        both = exact(d_odd * u_real, even)
        ops.append((split(jnp.concatenate([even, both], axis=0)), d_odd * u_twice))

    lane = lax.broadcasted_iota(jnp.int32, (4 * no, 4 * no), 1)
    line = lax.broadcasted_iota(jnp.int32, (4 * no, 4 * no), 0)
    here = jnp.where(line < 2 * no, line, line - no)
    unit_rows = jnp.logical_or(line < no, jnp.logical_and(line >= 2 * no, line < 3 * no))
    def grow(q, last):
        (a_hi, a_lo), odd_cols = ops[q]
        at = (q % 2) * 2 * no
        placed = jnp.where(jnp.logical_and(unit_rows, lane == here + at), 1.0, 0.0)
        span = lax.broadcasted_iota(jnp.int32, (2 * no, 4 * no), 1)
        kept = jnp.where(jnp.logical_and(span >= at, span < at + no), odd_cols, 0.0)
        placed = placed + jnp.concatenate([jnp.zeros_like(kept), kept], axis=0)
        if q == 0:
            block = placed
        else:
            high, low = last
            wide = mm(jnp.concatenate([a_hi, a_lo], axis=0), high)
            moved = wide[0 : 4 * no] + (wide[4 * no :] + mm(a_hi, low))
            if q % 2 == 0:
                block = jnp.concatenate([moved, placed], axis=1)
            else:
                width = moved.shape[1] - 4 * no
                tail = moved[:, width:] + placed
                block = tail if width == 0 else jnp.concatenate([moved[:, 0:width], tail], axis=1)
        width = block.shape[1]
        pmat[q, :, 0:width] = block.astype(BF16)
        if width < n_sa * rows:
            pmat[q, :, width:] = jnp.zeros((4 * no, n_sa * rows - width), BF16)
        return split(block[2 * no :])

    def send_moved():
        mine = ps.at[2 * me_tp + core]
        for k in range(1, n_tp):
            who = far(k)
            remote(pst.at[core], mine, s_p, r_p, (me_sa, who)).start()
            remote(pst.at[1 - core], mine, s_p, r_p, (sib, who)).start()
        remote(pst.at[1 - core], mine, s_p, r_p, (sib, me_tp)).start()

    def apply(left, right):
        moved = joined(*split_parts(mm(left, right), no)).astype(BF16)
        pst[0] = moved[0:rows]
        pst[1] = moved[rows:]
        send_moved()
        ps[2 * me_tp + core] = pst[core]

    def wait_pair(j):
        arrived(fall.at[2 * j : 2 * j + 2], r_f.at[j])

    def predict(begin, end):
        depth = end * rows
        left = pmat[begin:end, :, 0:depth].reshape((end - begin) * 2 * rows, depth)
        return joined(*split_parts(mm(left, fall[0:end].reshape(depth, cols)), no))

    def keep(x, begin, end):
        y2[core, begin:end] = x.astype(BF16).reshape(end - begin, rows, cols)

    wide = jnp.concatenate([factor2] * (n_sa // min(4, n_sa // 2)), axis=0)

    def spectral(x, begin, end):
        g = gall[begin:end].reshape((end - begin) * rows, cols).astype(F32)
        return spectral_packed(x, g, wide).astype(BF16)

    groups = min(4, n_sa // 2)
    pairs = n_sa // 2 // groups
    unit = 2 * pairs
    group = lax.div(pair, pairs)
    last = None
    for n in range(groups):
        for q in range(n * unit, (n + 1) * unit):
            last = grow(q, last)

        @pl.when(group == n)
        def _():
            arrived(gall.at[0 : n_sa - 1], r_g)
            arrived(fall.at[sib], r_f.at[pair])
            for j in range((n + 1) * pairs):
                pl.when(pair != j)(functools.partial(wait_pair, j))
            spans = [(m * unit, (m + 1) * unit) for m in range(n + 1)]
            tiles = [predict(*span) for span in spans]
            right = jnp.concatenate([spectral(x, *span) for x, span in zip(tiles, spans)], axis=0)
            apply(pmat[pl.ds(2 * pair, 2), :, 0 : right.shape[0]].reshape(4 * rows, -1), right)
            for x, span in zip(tiles, spans):
                keep(x, *span)

    for n in range(groups - 1):

        @pl.when(group == n)
        def _():
            for j in range((n + 1) * pairs, n_sa // 2):
                wait_pair(j)
            for m in range(n + 1, groups):
                span = (m * unit, (m + 1) * unit)
                keep(predict(*span), *span)

    remote(y2.at[core], y2.at[core], s_y, r_y, (sib, me_tp)).start()
    first_rows = jnp.concatenate([hist[h, 0, 0:no] for h in range(2)], axis=1).astype(F32)
    q_left = pmat[me_sa][:, 0:no]
    q_own = mm(q_left, begin(dall.at[0], first_rows).astype(BF16))
    q_own = joined_halves(*split_parts(q_own, no))

    arrived(y2.at[1 - core], r_y)
    def unpack(h0, h1):
        low = low_lanes(h0)
        return jnp.where(low, h0, swap(h1)), jnp.where(low, swap(h0), h1)

    y_re, y_im = unpack(*[y2[h].reshape(n_sa * rows, cols).astype(F32) for h in range(2)])
    for at, columns in ((0, (y_re, y_im)), (rows, (-y_im, y_re))):
        for h in range(2):
            block = columns[h].astype(BF16).reshape(n_sa, rows, cols)
            yst[:, at : at + rows, h * cols : (h + 1) * cols] = block
    base = unpack(*[
        0.5 * (y2[h, me_sa].astype(F32) + q_own[:, h * cols : (h + 1) * cols]) for h in range(2)
    ])

    left_here(spec1.at[0 : n_tp - 1], s_s)
    left_here(dall.at[0 : n_sa - 1, 0:1], s_d)
    left_here(yst.at[0 : n_sa - 1], s_h)
    left_here(ps.at[0 : 2 * n_tp - 1], s_p)
    left_here(y2.at[core], s_y)
    arrived(ps.at[0 : 2 * n_tp - 1], r_p)
    left = jnp.concatenate([ps[n] for n in range(2 * n_tp)], axis=1)
    final = (0.5 * scale) * mm(left, yst[...].reshape(2 * n_sa * rows, 2 * cols))
    for h in range(2):
        total = base[h] + final[:, h * cols : (h + 1) * cols]
        out[h] = total.reshape(win.shape[2], no, cols)


def shards(window, damping, propagator, coupling):
    n_sa, n_tp = lax.axis_size("sa"), lax.axis_size("tp")
    no = coupling.shape[0]
    block = window.shape[2]
    cols = window.shape[4]
    rows = block * no
    scale = 1.0 / (block * n_sa * math.sqrt(no))
    dma = lambda n: pltpu.SemaphoreType.DMA((n,))
    vm = pl.BlockSpec(memory_space=pltpu.VMEM)
    one = pltpu.SemaphoreType.DMA
    sems = [
        one, one, one, dma(n_sa // 2), one, one,
        one, one, dma(n_sa // 2), one, one, one, one,
    ]
    return pl.pallas_call(
        functools.partial(kernel, n_sa, n_tp, scale),
        out_shape=pltpu.VMEM((2, block, no, cols), F32),
        in_specs=[pl.BlockSpec(memory_space=pl.ANY)] * 4,
        out_specs=vm,
        scratch_shapes=[
            pltpu.VMEM(window.shape, F32),
            pltpu.VMEM(damping.shape, F32),
            pltpu.VMEM(propagator.shape, F32),
            pltpu.VMEM((1, no), F32),
            dma(4),
            pltpu.VMEM((n_sa, 8, 128), F32),
            pltpu.VMEM((2, n_sa, rows, cols), BF16),
            pltpu.VMEM((n_tp, 2 * rows, cols), BF16),
            pltpu.VMEM((2, rows, cols), BF16),
            pltpu.VMEM((n_sa, rows, cols), BF16),
            pltpu.VMEM((2, rows, cols), BF16),
            pltpu.VMEM((n_sa, rows, cols), BF16),
            pltpu.VMEM((n_sa, 2 * rows, n_sa * rows), BF16),
            pltpu.VMEM((2, rows, cols), BF16),
            pltpu.VMEM((2 * n_tp, rows, cols), BF16),
            pltpu.VMEM((2, n_sa, rows, cols), BF16),
            pltpu.VMEM((n_sa, 2 * rows, 2 * cols), BF16),
        ] + sems,
        compiler_params=pltpu.CompilerParams(collective_id=0, has_side_effects=True),
        name="kadanoff",
    )(window, damping, propagator, coupling.reshape(1, no))


def solution(mesh):
    return jax.shard_map(
        shards,
        mesh=mesh,
        in_specs=(P(None, None, "sa", None, "tp"), P("sa", None), P(), P()),
        out_specs=P(None, "sa", None, "tp"),
        check_vma=False,
    )
```
